128 devices in a mesh: grp: 16 (over x, z), sp: 8 (over y, core).
Axes of the slice: x: 4, y: 4, z: 4, core: 2. Of those that a mesh axis runs over, the one named last changes fastest.
Arguments:
- queries: bfloat16 [20480, 4096], P(('grp', 'sp')), may hold values from -128 to 128
- fresh_key_values: bfloat16 [20480, 1024], P(('grp', 'sp')), may hold values from -4 to 4
- cache: bfloat16 [16, 8, 256, 256], P('grp', 'sp'), may hold values from -4 to 4
- lengths: int32 [16, 8], P('grp', 'sp'), may hold values from 1 to 160, 1024 in all within a row
- out_weight: bfloat16 [4096, 2048], P('sp'), may hold values from -1 to 1
- residual: bfloat16 [20480, 2048], P(('grp', 'sp')), may hold values from -36 to 36
- norm_gain: float32 [2048], replicated, may hold values from 0.1 to 1.9
- expert_ids: int32 [20480, 8], P(('grp', 'sp')), may hold values from 0 to 127, all different within a row; in each aligned block of 160 rows (0 to 159, 160 to 319, ...) at most 16 rows name the same one
- gate_values: float32 [20480, 8], P(('grp', 'sp')), may hold values from 0.05 to 0.5
- up_gate_weight: bfloat16 [128, 2048, 1536], P(('grp', 'sp')), may hold values from -0.125 to 0.125
- down_weight: bfloat16 [128, 768, 2048], P(('grp', 'sp')), may hold values from -0.21875 to 0.21875
Outputs:
- attended: bfloat16 [20480, 2048], P(('grp', 'sp'))
- moe_out: bfloat16 [20480, 2048], P(('grp', 'sp'))
The draws below stay inside these ranges and needn't reach their ends.
Inputs may be any that keep to these rules, and one draw needn't show every extreme that they name: Each group's 8 lengths sum to 1024, and in every group one device has exactly 160. `expert_ids`: each slot names 8 different experts; among the 160 slots of one device no expert is named more than 16 times, and one expert is named exactly 16 times by the slots of some device.
All inputs are finite; a program needn't handle non-finite values.
Results may differ from the reference program's by a relative error of at most 0.02.
Values may be sent and summed in bfloat16 or wider, within the bound.
A program may use at most 128 MiB of HBM per device.

```python
import math
import jax
import jax.numpy as jnp
import numpy as np
from jax import lax

D = 2048
QUERY_HEADS = 32
KEY_VALUE_HEADS = 4
HEAD_SIZE = 128
FF = 768
TOPK = 8
CACHED_POSITIONS = 512
TOKEN_GROUPS = 16
GROUP_DEVICES = 8
E = 128
ROWS = 160
TOK_GRP = 1024
SLOTS_PER_GROUP = 1280
TOTAL_SLOTS = 20480
DEVICE_CACHE = 256
CAP = 16
DEVICES = 128


def cache_logical(key):
    starting_rows = jnp.clip(jax.random.normal(jax.random.fold_in(key, 701), (TOKEN_GROUPS, KEY_VALUE_HEADS, CACHED_POSITIONS, 2 * HEAD_SIZE), jnp.float32), -4.0, 4.0)
    return starting_rows


def draw_cache(key, part):
    return cache_logical(key).reshape(TOKEN_GROUPS, GROUP_DEVICES, DEVICE_CACHE, 2 * HEAD_SIZE).astype(jnp.bfloat16)


def draw_queries(key, part):
    query_key = jax.random.fold_in(key, 702)
    noise = jnp.clip(jax.random.normal(query_key, (TOTAL_SLOTS, QUERY_HEADS * HEAD_SIZE), jnp.float32), -4.0, 4.0) * 1.5
    return noise.astype(jnp.bfloat16)


def draw_residual(key, part):
    split_keys = jax.random.split(jax.random.fold_in(key, 703), 3)
    row_scale = jnp.exp(jax.random.uniform(split_keys[0], (TOTAL_SLOTS, 1), jnp.float32, minval=math.log(0.3), maxval=math.log(3.0)))
    col_scale = jnp.exp(jax.random.uniform(split_keys[1], (1, D), jnp.float32, minval=math.log(0.3), maxval=math.log(3.0)))
    core = jnp.clip(jax.random.normal(split_keys[2], (TOTAL_SLOTS, D), jnp.float32), -4.0, 4.0)
    return (core * row_scale * col_scale).astype(jnp.bfloat16)


def shard_levels(stream_key, dims, cuts, smallest, top_value):
    def one(axis_at, blocks):
        heights = jax.random.uniform(jax.random.fold_in(jax.random.fold_in(stream_key, 6), axis_at), (blocks,), jnp.float32, smallest / len(cuts), top_value / len(cuts))
        return jnp.repeat(jnp.exp(heights), dims[axis_at] // blocks).reshape((-1,) + (1,) * (len(dims) - axis_at - 1))

    level = one(*cuts[0])
    for cut in cuts[1:]:
        level = level * one(*cut)
    return level


def length_profile(amount, total, bound, skew):
    loads = [(1 << 20) // math.isqrt(standing ** skew) + 1 for standing in range(2, amount + 1)]
    spare, holding = total - bound - (amount - 1), [1] * (amount - 1)
    while spare > 0:
        candidates = [i for i in range(amount - 1) if holding[i] < bound]
        whole, budget = sum([loads[i] for i in candidates]), spare
        for i in candidates:
            extra = min(bound - holding[i], max(1, budget * loads[i] // whole), spare)
            holding[i] = holding[i] + extra
            spare = spare - extra
    return np.array([bound] + holding)


def ragged(rng, count, total, reach, lean):
    if count == 2:
        one = jax.random.randint(rng, (), max(1, total - reach), min(reach, total - 1) + 1)
        return jnp.stack([one, total - one])
    sizes = jnp.asarray(length_profile(count, total, reach, lean), jnp.int32)
    pairs = (count - 1) // 2
    donor, sink = sizes[1:1 + 2 * pairs:2], sizes[2:2 + 2 * pairs:2]
    slack = jnp.minimum(donor - 1, reach - sink)
    shifted = jax.random.randint(jax.random.fold_in(rng, 1), (pairs,), 0, 1 << 20) % (slack + 1)
    sizes = sizes.at[1:1 + 2 * pairs:2].set(donor - shifted).at[2:2 + 2 * pairs:2].set(sink + shifted)
    return sizes[jax.random.permutation(jax.random.fold_in(rng, 2), count)]


def assign_block(stream_key, own, number, rows, amount, top, most, lean):
    ranking = jax.random.permutation(stream_key, amount)
    packed, usual = shares(amount, rows * top, most, lean, True), shares(amount, rows * top, most, lean, False)
    places = jnp.arange(amount)

    def named(sizes, offset_by):
        used = int((sizes > 0).sum())
        fixed = max(1, used // 4)
        shifted = fixed + (places - fixed + offset_by * (used - fixed)) % max(1, amount - fixed)
        return jnp.zeros((amount,), jnp.int32).at[ranking[jnp.where(places < fixed, places, shifted)]].set(jnp.asarray(sizes, jnp.int32))

    sizes = jnp.where(number % 4 == 0, named(packed, number // 4), named(usual, number - number // 4 - 1))
    mixed = jax.random.permutation(jax.random.fold_in(own, 3), amount)
    giver, taker = mixed[0:amount // 2 * 2:2], mixed[1:amount // 2 * 2:2]
    slack = jnp.minimum(sizes[giver] - 1, most - sizes[taker]) // 2
    slack = jnp.where((giver == ranking[0]) | (taker == ranking[0]) | (sizes[taker] == 0), 0, jnp.maximum(slack, 0))
    shifted = jax.random.randint(jax.random.fold_in(own, 4), (amount // 2,), 0, 1 << 20) % (slack + 1)
    sizes = sizes.at[giver].add(-shifted).at[taker].add(shifted)
    labels = jnp.searchsorted(jnp.cumsum(sizes), jnp.arange(rows * top), side="right").astype(jnp.int32)
    table = labels.reshape(top, rows).T
    table = table[jax.random.permutation(jax.random.fold_in(own, 1), rows)]
    offset_by = jax.random.randint(jax.random.fold_in(own, 2), (rows, 1), 0, top)
    return jnp.take_along_axis(table, (jnp.arange(top)[None, :] + offset_by) % top, axis=1)


def shares(amount, total, reach, slope, full):
    weights = [(1 << 20) // math.isqrt(standing ** slope) + 1 for standing in range(1, amount + 1)]
    largest = reach if full else min(reach, max(-(-total // amount), total * weights[0] // sum(weights)))
    least = 1 if total - largest >= amount - 1 else 0
    counts, spare = [largest] + [least] * (amount - 1), total - largest - least * (amount - 1)
    while spare > 0:
        free = [i for i in range(1, amount) if counts[i] < largest] or [i for i in range(1, amount) if counts[i] < reach]
        pool, budget = sum([weights[i] for i in free]), spare
        for i in free:
            extra = min(reach - counts[i], max(1, budget * weights[i] // pool), spare)
            counts[i] = counts[i] + extra
            spare = spare - extra
    return np.array(counts)


def bell_draw(key, extent, deviation, limit, cuts=(), held_as=jnp.bfloat16):
    loudness = shard_levels(key, extent, cuts, -0.22, 0.18) if cuts else 1.0
    result = jax.random.normal(key, extent, jnp.float32) * deviation * loudness
    return jnp.minimum(jnp.maximum(result, -limit), limit).astype(held_as)


def setup_inputs(seed: int = 0) -> dict:
    key_list = jax.random.split(jax.random.key(seed), 12)
    queries = draw_queries(jax.random.fold_in(key_list[11], 71), 0)
    fresh_key_values = bell_draw(key_list[1], (TOTAL_SLOTS, 2 * KEY_VALUE_HEADS * HEAD_SIZE), 1.0, 4.0, ((0, 128),))
    cache = draw_cache(jax.random.fold_in(key_list[11], 71), 0)
    lengths = jax.vmap(lambda own: ragged(own, GROUP_DEVICES, TOK_GRP, ROWS, 2))(jax.random.split(key_list[3], TOKEN_GROUPS)).reshape((TOKEN_GROUPS, GROUP_DEVICES)).astype(jnp.int32)
    out_weight = bell_draw(key_list[4], (QUERY_HEADS * HEAD_SIZE, D), 0.0625, 1.0, ((0, 8),))
    residual = draw_residual(jax.random.fold_in(key_list[11], 71), 0)
    norm_gain = jnp.clip(1.0 + 0.18 * jax.random.normal(key_list[6], (D,), jnp.float32), 0.1, 1.9)
    expert_ids_keys = jax.random.split(jax.random.fold_in(key_list[7], 1), TOTAL_SLOTS // ROWS)
    expert_ids_turns = jax.random.permutation(jax.random.fold_in(key_list[7], 3), TOTAL_SLOTS // ROWS)
    expert_ids = jax.vmap(lambda own, number: assign_block(jax.random.fold_in(key_list[7], 2), own, number, ROWS, E, TOPK, CAP, 2))(expert_ids_keys, expert_ids_turns).reshape((TOTAL_SLOTS, TOPK))
    gate_values = jnp.clip(jnp.exp(math.log(0.5) - 2.3025851 * jax.random.uniform(key_list[8], (TOTAL_SLOTS, TOPK), jnp.float32) ** shard_levels(key_list[8], (TOTAL_SLOTS, TOPK), ((0, 128),), -0.2, 0.2)), 0.05, 0.5)
    up_gate_weight = bell_draw(key_list[9], (E, D, 2 * FF), D ** -0.5, 0.125, ((0, 128),))
    down_weight = bell_draw(key_list[10], (E, FF, D), FF ** -0.5, 0.21875, ((0, 128),))
    return {"queries": queries, "fresh_key_values": fresh_key_values, "cache": cache, "lengths": lengths, "out_weight": out_weight, "residual": residual, "norm_gain": norm_gain, "expert_ids": expert_ids, "gate_values": gate_values, "up_gate_weight": up_gate_weight, "down_weight": down_weight}


def attend_group(inputs, out_weight):
    rows_of_queries, key_value_rows, cached_rows, stretch_lens = inputs
    rows_of_group = rows_of_queries.shape[0]
    queries_per_key_head = QUERY_HEADS // KEY_VALUE_HEADS
    stretch_lens = stretch_lens.astype(jnp.int32)
    offsets = (jnp.cumsum(stretch_lens) - stretch_lens).astype(jnp.int32)
    slot_ids = jnp.arange(rows_of_group, dtype=jnp.int32)
    source = slot_ids // ROWS
    within = slot_ids % ROWS
    is_live = within < stretch_lens[source]
    position = offsets[source] + within
    allowed = is_live[None, :] & (position[None, :] <= position[:, None])
    visible = jnp.concatenate([jnp.ones((rows_of_group, CACHED_POSITIONS), dtype=bool), allowed], axis=1)
    cached_heads = cached_rows.reshape(KEY_VALUE_HEADS, CACHED_POSITIONS, 2 * HEAD_SIZE)
    queries_by_head = rows_of_queries.reshape(rows_of_group, KEY_VALUE_HEADS, queries_per_key_head, HEAD_SIZE).transpose(1, 2, 0, 3)
    fresh_keys = key_value_rows[:, :KEY_VALUE_HEADS * HEAD_SIZE].reshape(rows_of_group, KEY_VALUE_HEADS, HEAD_SIZE).transpose(1, 0, 2)
    fresh_values = key_value_rows[:, KEY_VALUE_HEADS * HEAD_SIZE:].reshape(rows_of_group, KEY_VALUE_HEADS, HEAD_SIZE).transpose(1, 0, 2)

    def one_head(parts):
        query_part, key_new, value_new, cache_part = parts
        key_all = jnp.concatenate([cache_part[:, :HEAD_SIZE], key_new], axis=0).astype(jnp.float32)
        value_all = jnp.concatenate([cache_part[:, HEAD_SIZE:], value_new], axis=0).astype(jnp.float32)
        scores = jnp.einsum('grd,kd->grk', query_part.astype(jnp.float32), key_all) / math.sqrt(HEAD_SIZE)
        scores = jnp.where(visible[None], scores, -jnp.inf)
        row_max = lax.optimization_barrier(jnp.max(scores, axis=-1, keepdims=True))
        weights = jnp.exp(scores - row_max)
        totals = lax.optimization_barrier(jnp.sum(weights, axis=-1, keepdims=True))
        probs = lax.optimization_barrier(weights.astype(jnp.bfloat16)).astype(jnp.float32)
        return (jnp.einsum('grk,kd->grd', probs, value_all) / totals).astype(jnp.bfloat16)
    results = lax.map(one_head, (queries_by_head, fresh_keys, fresh_values, cached_heads))
    heads = results.reshape(QUERY_HEADS, rows_of_group, HEAD_SIZE).transpose(1, 0, 2).reshape(rows_of_group, QUERY_HEADS * HEAD_SIZE)
    return (jnp.dot(heads, out_weight, preferred_element_type=jnp.float32), is_live)

def reference(queries, fresh_key_values, cache, lengths, out_weight, residual, norm_gain, expert_ids, gate_values, up_gate_weight, down_weight):

    def group_labour(parts):
        return attend_group(parts, out_weight)
    attention_groups, active_groups = lax.map(group_labour, (queries.reshape(TOKEN_GROUPS, SLOTS_PER_GROUP, QUERY_HEADS * HEAD_SIZE), fresh_key_values.reshape(TOKEN_GROUPS, SLOTS_PER_GROUP, 2 * KEY_VALUE_HEADS * HEAD_SIZE), cache.reshape(TOKEN_GROUPS, GROUP_DEVICES * DEVICE_CACHE, 2 * HEAD_SIZE), lengths))
    attn_sum = attention_groups.reshape(TOTAL_SLOTS, D)
    is_live = active_groups.reshape(TOTAL_SLOTS)
    attended = jnp.where(is_live[:, None], attn_sum, 0.0).astype(jnp.bfloat16)
    mixed_rows = residual.astype(jnp.float32) + attn_sum
    normed = (mixed_rows * lax.rsqrt(lax.optimization_barrier(jnp.mean(mixed_rows * mixed_rows, axis=-1, keepdims=True)) + 1e-06) * norm_gain).astype(jnp.bfloat16)
    route_ids = expert_ids.reshape(DEVICES, ROWS, TOPK)
    live_dev = is_live.reshape(DEVICES, ROWS)
    expert_range = jnp.arange(E, dtype=jnp.int32)
    chosen = jnp.any(route_ids[..., None] == expert_range, axis=2) & live_dev[..., None]
    counted = chosen.astype(jnp.int32)
    prefix = (jnp.cumsum(counted, axis=1) - counted).astype(jnp.int32)
    slot_in = jnp.take_along_axis(prefix, route_ids, axis=2).astype(jnp.int32)
    device_ids = jnp.arange(DEVICES, dtype=jnp.int32)[:, None, None]
    table_size = E * DEVICES * CAP
    target = jnp.where(live_dev[..., None], route_ids * (DEVICES * CAP) + device_ids * CAP + slot_in, table_size).reshape(-1).astype(jnp.int32)
    token_ids = jnp.broadcast_to(jnp.arange(TOTAL_SLOTS, dtype=jnp.int32).reshape(DEVICES, ROWS, 1), route_ids.shape).reshape(-1)
    token_table = jnp.full((table_size + 1,), TOTAL_SLOTS, dtype=jnp.int32).at[target].set(token_ids)[:table_size].reshape(E, DEVICES * CAP)
    gate_table = jnp.zeros((table_size + 1,), jnp.float32).at[target].set(gate_values.reshape(-1))[:table_size].reshape(E, DEVICES * CAP)
    padded = jnp.concatenate([normed, jnp.zeros((1, D), jnp.bfloat16)], axis=0)

    def one_expert(accum, parts):
        token_col, gate_col, up_gate, down_part = parts
        rows_in = padded[token_col]
        projected = jnp.dot(rows_in, up_gate, preferred_element_type=jnp.float32)
        hidden = (jax.nn.silu(projected[:, :FF]) * projected[:, FF:]).astype(jnp.bfloat16)
        expert_out = jnp.dot(hidden, down_part, preferred_element_type=jnp.float32).astype(jnp.bfloat16)
        return (accum.at[token_col].add(gate_col[:, None] * expert_out.astype(jnp.float32)), None)
    accum = lax.scan(one_expert, jnp.zeros((TOTAL_SLOTS + 1, D), jnp.float32), (token_table, gate_table, up_gate_weight, down_weight))[0]
    moe_out = jnp.where(is_live[:, None], accum[:TOTAL_SLOTS], 0.0).astype(jnp.bfloat16)
    return (attended, moe_out)
```

```python
import math

import jax
import jax.numpy as jnp
from jax import lax
from jax.sharding import PartitionSpec as P


def from_everyone(x, axis):
    devices = lax.axis_size(axis)
    return lax.all_to_all(jnp.broadcast_to(x[None], (devices, *x.shape)), axis, 0, 0, tiled=True)


def in_order(pieces, dim):
    shape = list(pieces.shape[1:])
    shape[dim] *= pieces.shape[0]
    return jnp.moveaxis(pieces, 0, dim).reshape(shape)


def gather_directly(x, axis, dim):
    pieces = from_everyone(x, axis)
    return in_order(pieces, dim)


def partner_2(value, axis, bit):
    mask = 2**bit
    pairs = [(source, source ^ mask) for source in range(lax.axis_size(axis))]
    return lax.ppermute(value, axis, pairs)


def split_up(x, dim, devices):
    before, after = (x.shape[:dim], x.shape[dim + 1 :])
    return jnp.moveaxis(x.reshape(*before, devices, -1, *after), dim, 0)


def exchange_both(x, axis, axes, splits, concats):
    sizes = [lax.axis_size(a) for a in axes]
    pieces = split_up(x, splits[0], sizes[0])
    pieces = jnp.moveaxis(split_up(pieces, splits[1] + 1, sizes[1]), 0, 1)
    inside = pieces.shape[2:]
    pieces = pieces.reshape(-1, *inside)
    pieces = lax.all_to_all(pieces, axis, split_axis=0, concat_axis=0, tiled=True)
    pieces = in_order(pieces.reshape(*sizes, *inside), concats[0] + 1)
    return in_order(pieces, concats[1])


def per_device(
    queries,
    fresh_key_values,
    cache,
    lengths,
    out_weight,
    residual,
    norm_gain,
    expert_ids,
    gate_values,
    up_gate_weight,
    down_weight,
):
    seq_devices = lax.axis_size("sp")
    slot_rows = queries.shape[0]
    head_width = cache.shape[-1] // 2
    model_width = residual.shape[1]
    kv_heads = fresh_key_values.shape[1] // (2 * head_width)
    repeat = seq_devices // kv_heads
    keys_new = fresh_key_values[:, : kv_heads * head_width].reshape(
        slot_rows, kv_heads, 1, head_width
    )
    values_new = fresh_key_values[:, kv_heads * head_width :].reshape(
        slot_rows, kv_heads, 1, head_width
    )
    paired = jnp.concatenate([keys_new, values_new], axis=3)
    spread = jnp.broadcast_to(paired, (slot_rows, kv_heads, repeat, 2 * head_width)).reshape(
        slot_rows, seq_devices * 2 * head_width
    )
    all_lengths = gather_directly(lengths, "sp", 1)
    queries_by_head, head_kv = (
        lax.all_to_all(queries, "sp", split_axis=1, concat_axis=0, tiled=True),
        lax.all_to_all(spread, "sp", split_axis=1, concat_axis=0, tiled=True),
    )
    cache_block = cache[0, 0]
    my_index = lax.axis_index("sp")
    partner = partner_2(cache_block, "sp", 0)
    is_upper = my_index // 2**0 % 2 == 1
    cache_block = jnp.where(
        is_upper,
        jnp.concatenate([partner, cache_block], axis=0),
        jnp.concatenate([cache_block, partner], axis=0),
    )
    stretch_lens = all_lengths[0]
    offsets = jnp.cumsum(stretch_lens) - stretch_lens
    rows_of_group = queries_by_head.shape[0]
    slot_ids = jnp.arange(rows_of_group, dtype=jnp.int32)
    source = slot_ids // slot_rows
    within = slot_ids % slot_rows
    from_device = source[:, None] == jnp.arange(seq_devices, dtype=jnp.int32)[None, :]
    is_live = within < jnp.sum(jnp.where(from_device, stretch_lens[None, :], 0), axis=1)
    position = within + jnp.sum(jnp.where(from_device, offsets[None, :], 0), axis=1)
    per_dev = queries_by_head.shape[1] // head_width
    cache_len = cache_block.shape[0]
    key_all = jnp.concatenate([cache_block[:, :head_width], head_kv[:, :head_width]], axis=0)
    value_all = jnp.concatenate([cache_block[:, head_width:], head_kv[:, head_width:]], axis=0)
    block_count = 2
    block_rows = rows_of_group // block_count

    def attend(parts):
        query_block, place_block = parts
        scores = jnp.einsum(
            "rhd,kd->hrk", query_block, key_all, preferred_element_type=jnp.float32
        ) / math.sqrt(head_width)
        allowed = jnp.concatenate(
            [
                jnp.ones((block_rows, cache_len), dtype=bool),
                is_live[None, :] & (position[None, :] <= place_block[:, None]),
            ],
            axis=1,
        )
        scores = jnp.where(allowed[None], scores, -jnp.inf)
        row_max = jnp.max(scores, axis=-1, keepdims=True)
        weights = jnp.exp(scores - row_max)
        totals = jnp.sum(weights, axis=-1, keepdims=True)
        result = (
            jnp.einsum(
                "hrk,kd->hrd",
                weights.astype(jnp.bfloat16),
                value_all,
                preferred_element_type=jnp.float32,
            )
            / totals
        )
        return (
            result.astype(jnp.bfloat16).transpose(1, 0, 2).reshape(block_rows, per_dev * head_width)
        )

    attn_heads = lax.map(
        attend,
        (
            queries_by_head.reshape(block_count, block_rows, per_dev, head_width),
            position.reshape(block_count, block_rows),
        ),
    ).reshape(rows_of_group, per_dev * head_width)
    attn_sum = lax.psum_scatter(
        jnp.dot(attn_heads, out_weight, preferred_element_type=jnp.float32).astype(jnp.bfloat16),
        "sp",
        scatter_dimension=0,
        tiled=True,
    ).astype(jnp.float32)
    own_live = jnp.arange(slot_rows, dtype=jnp.int32) < lengths[0, 0]
    attended = jnp.where(own_live[:, None], attn_sum, 0.0).astype(jnp.bfloat16)
    mixed_rows = residual.astype(jnp.float32) + attn_sum
    normed = (
        mixed_rows
        * lax.rsqrt(jnp.mean(mixed_rows * mixed_rows, axis=-1, keepdims=True) + 1e-06)
        * norm_gain
    ).astype(jnp.bfloat16)
    group_count = lax.axis_size("grp")
    experts = up_gate_weight.shape[0] * group_count * seq_devices
    top_count = expert_ids.shape[1]
    capacity = max(2, 8 * slot_rows * top_count // (5 * experts))
    hidden_width = down_weight.shape[1]
    choose = expert_ids[:, :, None] == jnp.arange(experts, dtype=jnp.int32)[None, None, :]
    routed = (jnp.any(choose, axis=1) & own_live[:, None]).astype(jnp.float32)
    earlier = (jnp.arange(slot_rows)[:, None] > jnp.arange(slot_rows)[None, :]).astype(jnp.float32)
    prefix = jnp.dot(earlier, routed, precision=lax.Precision.HIGHEST)
    slot_in = jnp.sum(jnp.where(choose, prefix[:, None, :], 0.0), axis=2).astype(jnp.int32)
    dump_slot = experts * capacity
    target = jnp.where(own_live[:, None], expert_ids * capacity + slot_in, dump_slot)
    slot_range = jnp.arange(dump_slot, dtype=jnp.int32)
    hits = target.T[:, None, :] == slot_range[None, :, None]
    select = jnp.any(hits, axis=0).astype(jnp.bfloat16)
    outgoing = jnp.dot(select, normed, preferred_element_type=jnp.float32).astype(jnp.bfloat16)
    sectioned = outgoing.reshape(group_count, seq_devices, capacity, model_width)
    arrived = exchange_both(sectioned, ("grp", "sp"), ("grp", "sp"), (0, 1), (0, 1))
    flat_rows = arrived.reshape(-1, model_width)
    projected = jnp.dot(flat_rows, up_gate_weight[0], preferred_element_type=jnp.float32)
    hidden = (jax.nn.silu(projected[:, :hidden_width]) * projected[:, hidden_width:]).astype(
        jnp.bfloat16
    )
    returned = exchange_both(
        jnp.dot(hidden, down_weight[0], preferred_element_type=jnp.float32)
        .astype(jnp.bfloat16)
        .reshape(arrived.shape),
        ("grp", "sp"),
        ("grp", "sp"),
        (0, 1),
        (0, 1),
    )
    matches = target[:, :, None] == slot_range[None, None, :]
    mixing = jnp.sum(jnp.where(matches, gate_values[:, :, None], 0.0), axis=1)
    combined = jnp.dot(
        mixing.astype(jnp.bfloat16),
        returned.reshape(dump_slot, model_width),
        preferred_element_type=jnp.float32,
    )
    moe_out = jnp.where(own_live[:, None], combined, 0.0).astype(jnp.bfloat16)
    return (attended, moe_out)


def solution(mesh):
    in_specs = (
        P(("grp", "sp"), None),
        P(("grp", "sp"), None),
        P("grp", "sp", None, None),
        P("grp", "sp"),
        P("sp", None),
        P(("grp", "sp"), None),
        P(),
        P(("grp", "sp"), None),
        P(("grp", "sp"), None),
        P(("grp", "sp"), None, None),
        P(("grp", "sp"), None, None),
    )
    out_specs = (P(("grp", "sp"), None), P(("grp", "sp"), None))
    return jax.shard_map(
        per_device, mesh=mesh, in_specs=in_specs, out_specs=out_specs, check_vma=False
    )
```

```python
import functools
import math

import jax
import jax.numpy as jnp
from jax import lax
from jax.experimental import pallas as pl
from jax.experimental.pallas import tpu as pltpu
from jax.sharding import PartitionSpec as P


def in_order(pieces, dim):
    shape = list(pieces.shape[1:])
    shape[dim] *= pieces.shape[0]
    return jnp.moveaxis(pieces, 0, dim).reshape(shape)


def split_up(x, dim, devices):
    before, after = (x.shape[:dim], x.shape[dim + 1 :])
    return jnp.moveaxis(x.reshape(*before, devices, -1, *after), dim, 0)


def exchange_both(x, axis, axes, splits, concats):
    sizes = [lax.axis_size(a) for a in axes]
    pieces = split_up(x, splits[0], sizes[0])
    pieces = jnp.moveaxis(split_up(pieces, splits[1] + 1, sizes[1]), 0, 1)
    inside = pieces.shape[2:]
    pieces = pieces.reshape(-1, *inside)
    pieces = lax.all_to_all(pieces, axis, split_axis=0, concat_axis=0, tiled=True)
    pieces = in_order(pieces.reshape(*sizes, *inside), concats[0] + 1)
    return in_order(pieces, concats[1])


MESH = pl.DeviceIdType.MESH
NEG = -1e30


def group_attention(
    q_hbm, fkv_hbm, cache_hbm, lens_ref, w_hbm, res_hbm, gain_ref,
    attended_ref, normed_ref,
    qb, kx, vx, lb, w, res, heads, own_part, give, take, relay, half_in, full_in,
    q_send, k_send, v_send, l_send, q_recv, k_recv, v_recv, l_recv,
    c_send, c_recv, local, pair_send, pair_recv, ring_send, ring_recv,
):
    me = lax.axis_index("sp")
    devices = qb.shape[0]
    rows, wide = qb.shape[1], qb.shape[2]
    depth = kx.shape[1] // 2
    per = wide // depth
    block = cache_hbm.shape[0]
    cached = 2 * block
    chips = devices // 2
    y, c = me // 2, lax.rem(me, 2)
    partner = y * 2 + 1 - c
    width = w.shape[1]
    half = width // 2

    bar = pltpu.get_barrier_semaphore()
    for i in range(1, devices):
        pl.semaphore_signal(
            bar, inc=1, device_id={"sp": lax.rem(me + i, devices)}, device_id_type=MESH
        )

    local_copies = [
        pltpu.make_async_copy(w_hbm, w, local.at[0]),
        pltpu.make_async_copy(res_hbm, res, local.at[1]),
        pltpu.make_async_copy(
            cache_hbm.at[:, pl.ds(0, depth)],
            kx.at[pl.ds(c * block, block), pl.ds(0, depth)],
            local.at[2],
        ),
        pltpu.make_async_copy(
            cache_hbm.at[:, pl.ds(depth, depth)],
            vx.at[pl.ds(c * block, block), pl.ds(0, depth)],
            local.at[3],
        ),
        pltpu.make_async_copy(
            fkv_hbm.at[:, pl.ds(y * depth, depth)],
            kx.at[pl.ds(cached + me * rows, rows), pl.ds(0, depth)],
            local.at[4],
        ),
        pltpu.make_async_copy(
            fkv_hbm.at[:, pl.ds((chips + y) * depth, depth)],
            vx.at[pl.ds(cached + me * rows, rows), pl.ds(0, depth)],
            local.at[5],
        ),
        pltpu.make_async_copy(q_hbm.at[:, pl.ds(me * wide, wide)], qb.at[me], local.at[6]),
        pltpu.make_async_copy(lens_ref, lb.at[me], local.at[7]),
    ]
    for copy in local_copies:
        copy.start()

    vx[:, depth:] = jnp.ones((vx.shape[0], depth), jnp.bfloat16)
    kx[:cached, depth:] = jnp.zeros((cached, depth), jnp.bfloat16)

    pl.semaphore_wait(bar, devices - 1)

    def k_copy(i):
        p = lax.rem(me + i, devices)
        return pltpu.make_async_remote_copy(
            fkv_hbm.at[:, pl.ds((p // 2) * depth, depth)],
            kx.at[pl.ds(cached + me * rows, rows), pl.ds(0, depth)],
            k_send.at[i], k_recv.at[i], device_id={"sp": p}, device_id_type=MESH,
        )

    def v_copy(i):
        p = lax.rem(me + i, devices)
        return pltpu.make_async_remote_copy(
            fkv_hbm.at[:, pl.ds((chips + p // 2) * depth, depth)],
            vx.at[pl.ds(cached + me * rows, rows), pl.ds(0, depth)],
            v_send.at[i], v_recv.at[i], device_id={"sp": p}, device_id_type=MESH,
        )

    def l_copy(i):
        p = lax.rem(me + i, devices)
        return pltpu.make_async_remote_copy(
            lens_ref, lb.at[me], l_send.at[i], l_recv.at[i],
            device_id={"sp": p}, device_id_type=MESH,
        )

    def q_copy(p):
        return pltpu.make_async_remote_copy(
            q_hbm.at[:, pl.ds(p * wide, wide)], qb.at[me], q_send.at[p], q_recv.at[me],
            device_id={"sp": p}, device_id_type=MESH,
        )

    cache_copies = [
        pltpu.make_async_remote_copy(
            cache_hbm.at[:, pl.ds(d * depth, depth)],
            dst.at[pl.ds(c * block, block), pl.ds(0, depth)],
            c_send.at[d], c_recv.at[d], device_id={"sp": partner}, device_id_type=MESH,
        )
        for d, dst in enumerate((kx, vx))
    ]
    far_first = (4, 5, 3, 2, 6, 1, 7)
    for i in far_first:
        k_copy(i).start()
        v_copy(i).start()
        l_copy(i).start()
    for copy in cache_copies:
        copy.start()
    q_copy(partner).start()
    for dy in (2, 1, 3):
        for cc in range(2):
            q_copy(lax.rem(y + dy, chips) * 2 + cc).start()

    for copy in local_copies:
        copy.wait()
    for copy in cache_copies:
        copy.wait_recv()
    for i in range(1, devices):
        l_copy(i).wait_recv()
        k_copy(i).wait_recv()
        v_copy(i).wait_recv()
    row_ids = lax.broadcasted_iota(jnp.int32, (rows, depth), 0)
    for t in range(devices):
        alive = row_ids < lb[t, 0:1, :]
        kx[cached + t * rows : cached + (t + 1) * rows, depth:] = jnp.where(
            alive, 0.0, NEG
        ).astype(jnp.bfloat16)

    scale = math.log2(math.e) / math.sqrt(depth)
    pair_rows = 2 * rows
    lane = lax.broadcasted_iota(jnp.int32, (pair_rows, depth), 1)
    pick = jnp.where(lane == 0, 1.0, 0.0).astype(jnp.bfloat16)

    def attend(chip):
        keys = cached + (chip + 1) * pair_rows
        first = (cached + chip * pair_rows) // 128 * 128
        shift = cached + chip * pair_rows - first

        def head(h, carry):
            q = qb[2 * chip : 2 * chip + 2, :, pl.ds(pl.multiple_of(h * depth, depth), depth)]
            q = jnp.concatenate([q.reshape(pair_rows, depth), pick], axis=1)
            dims = (((1,), (1,)), ((), ()))
            sa = lax.dot_general(q, kx[:first, :], dims, preferred_element_type=jnp.float32)
            sb = lax.dot_general(q, kx[first:keys, :], dims, preferred_element_type=jnp.float32)
            i = lax.broadcasted_iota(jnp.int32, sb.shape, 0)
            j = lax.broadcasted_iota(jnp.int32, sb.shape, 1)
            sb = jnp.where(j - shift <= i, sb, NEG)
            top = jnp.maximum(
                jnp.max(sa, axis=1, keepdims=True), jnp.max(sb, axis=1, keepdims=True)
            )
            pa = jnp.exp2((sa - top) * scale).astype(jnp.bfloat16)
            pb = jnp.exp2((sb - top) * scale).astype(jnp.bfloat16)
            out = jnp.dot(pa, vx[:first, :], preferred_element_type=jnp.float32)
            out = out + jnp.dot(pb, vx[first:keys, :], preferred_element_type=jnp.float32)
            heads[:, pl.ds(pl.multiple_of(h * depth, depth), depth)] = (
                out[:, :depth] / out[:, depth:]
            ).astype(jnp.bfloat16)
            return carry

        lax.fori_loop(0, per, head, 0)

    def pair_copy(slot):
        return pltpu.make_async_remote_copy(
            give.at[slot], take.at[slot], pair_send.at[slot], pair_recv.at[slot],
            device_id={"sp": partner}, device_id_type=MESH,
        )

    up = lax.rem(y + 1, chips) * 2 + c
    down = lax.rem(y + chips - 1, chips) * 2 + c

    def ring_copy(n):
        src, dst, to = (
            (relay.at[0, :, pl.ds(0, half)], half_in.at[0], up),
            (relay.at[0, :, pl.ds(half, half)], half_in.at[1], down),
            (relay.at[1], full_in.at[0], up),
            (relay.at[2], full_in.at[1], down),
        )[n]
        return pltpu.make_async_remote_copy(
            src, dst, ring_send.at[n], ring_recv.at[n],
            device_id={"sp": to}, device_id_type=MESH,
        )

    def project(side, store):
        mine = heads[pl.ds(pl.multiple_of(side * rows, rows), rows), :]
        for n in range(4):
            cols = slice(n * (width // 4), (n + 1) * (width // 4))
            store(cols, jnp.dot(mine, w[:, cols], preferred_element_type=jnp.float32))

    def step(n, carry):
        dy = jnp.where(n == 3, 3, lax.rem(n * 2, 3))
        chip = lax.rem(y + dy, chips)

        @pl.when(n > 0)
        def _():
            for cc in range(2):
                t = chip * 2 + cc
                pltpu.make_async_copy(qb.at[t], qb.at[t], q_recv.at[t]).wait()

        @pl.when(n == 0)
        def _():
            pltpu.make_async_copy(qb.at[partner], qb.at[partner], q_recv.at[partner]).wait()

        lax.switch(chip, [functools.partial(attend, k) for k in range(chips)])

        def to_give(cols, value):
            give[n, :, cols] = value.astype(jnp.bfloat16)

        def to_own(cols, value):
            own_part[n, :, cols] = value

        project(1 - c, to_give)
        pair_copy(n).start()
        project(c, to_own)

        @pl.when(n == 1)
        def _():
            pair_copy(1).wait_recv()
            relay[0] = (own_part[1] + take[1].astype(jnp.float32)).astype(jnp.bfloat16)
            ring_copy(0).start()
            ring_copy(1).start()

        @pl.when(n == 2)
        def _():
            pair_copy(2).wait_recv()
            ring_copy(0).wait_recv()
            relay[1, :, :half] = (
                own_part[2, :, :half]
                + take[2, :, :half].astype(jnp.float32)
                + half_in[0].astype(jnp.float32)
            ).astype(jnp.bfloat16)
            relay[1, :, half:] = (
                own_part[2, :, half:] + take[2, :, half:].astype(jnp.float32)
            ).astype(jnp.bfloat16)
            ring_copy(2).start()

        @pl.when(n == 3)
        def _():
            pair_copy(3).wait_recv()
            ring_copy(1).wait_recv()
            relay[2, :, :half] = (
                own_part[3, :, :half] + take[3, :, :half].astype(jnp.float32)
            ).astype(jnp.bfloat16)
            relay[2, :, half:] = (
                own_part[3, :, half:]
                + take[3, :, half:].astype(jnp.float32)
                + half_in[1].astype(jnp.float32)
            ).astype(jnp.bfloat16)
            ring_copy(3).start()

        return carry

    lax.fori_loop(0, chips, step, 0)
    pair_copy(0).wait_recv()
    own_part[0] = own_part[0] + take[0].astype(jnp.float32)
    ring_copy(2).wait_recv()
    own_part[0] = own_part[0] + full_in[0].astype(jnp.float32)
    ring_copy(3).wait_recv()
    total = own_part[0] + full_in[1].astype(jnp.float32)
    alive = lax.broadcasted_iota(jnp.int32, (rows, 128), 0) < lens_ref[0:1, :]
    keep = jnp.max(jnp.where(alive, 1.0, 0.0), axis=1, keepdims=True)
    attended_ref[...] = jnp.where(keep > 0.0, total, 0.0).astype(jnp.bfloat16)
    mixed = res[...].astype(jnp.float32) + total
    power = jnp.mean(mixed * mixed, axis=1, keepdims=True)
    normed_ref[...] = (mixed * lax.rsqrt(power + 1e-06) * gain_ref[...]).astype(jnp.bfloat16)

    for i in range(1, devices):
        k_copy(i).wait_send()
        v_copy(i).wait_send()
        l_copy(i).wait_send()
        q_copy(lax.rem(me + i, devices)).wait_send()
    for copy in cache_copies:
        copy.wait_send()
    for n in range(4):
        pair_copy(n).wait_send()
        ring_copy(n).wait_send()


def attention(queries, fresh_key_values, cache, lengths, out_weight, residual, norm_gain):
    devices = lax.axis_size("sp")
    rows, wide = queries.shape[0], queries.shape[1] // devices
    block, depth = cache.shape[2], cache.shape[3] // 2
    width = residual.shape[1]
    keys = 2 * block + devices * rows
    any_spec = pl.BlockSpec(memory_space=pl.ANY)
    vmem = pl.BlockSpec(memory_space=pltpu.VMEM)
    dma = pltpu.SemaphoreType.DMA
    out = jax.ShapeDtypeStruct((rows, width), jnp.bfloat16)
    return pl.pallas_call(
        group_attention,
        out_shape=(out, out),
        in_specs=[any_spec, any_spec, any_spec, vmem, any_spec, any_spec, vmem],
        out_specs=(vmem, vmem),
        scratch_shapes=[
            pltpu.VMEM((devices, rows, wide), jnp.bfloat16),
            pltpu.VMEM((keys, 2 * depth), jnp.bfloat16),
            pltpu.VMEM((keys, 2 * depth), jnp.bfloat16),
            pltpu.VMEM((devices, 8, 128), jnp.int32),
            pltpu.VMEM(out_weight.shape, jnp.bfloat16),
            pltpu.VMEM((rows, width), jnp.bfloat16),
            pltpu.VMEM((2 * rows, wide), jnp.bfloat16),
            pltpu.VMEM((4, rows, width), jnp.float32),
            pltpu.VMEM((4, rows, width), jnp.bfloat16),
            pltpu.VMEM((4, rows, width), jnp.bfloat16),
            pltpu.VMEM((3, rows, width), jnp.bfloat16),
            pltpu.VMEM((2, rows, width // 2), jnp.bfloat16),
            pltpu.VMEM((2, rows, width), jnp.bfloat16),
            dma((devices,)), dma((devices,)), dma((devices,)), dma((devices,)),
            dma((devices,)), dma((devices,)), dma((devices,)), dma((devices,)),
            dma((2,)), dma((2,)), dma((8,)), dma((4,)), dma((4,)), dma((4,)), dma((4,)),
        ],
        compiler_params=pltpu.CompilerParams(
            collective_id=0, has_side_effects=True, vmem_limit_bytes=56 * 1024 * 1024
        ),
    )(
        queries,
        fresh_key_values,
        cache[0, 0],
        jnp.broadcast_to(lengths, (8, 128)),
        out_weight,
        residual,
        norm_gain[None, :],
    )


def per_device(
    queries,
    fresh_key_values,
    cache,
    lengths,
    out_weight,
    residual,
    norm_gain,
    expert_ids,
    gate_values,
    up_gate_weight,
    down_weight,
):
    seq_devices = lax.axis_size("sp")
    slot_rows = queries.shape[0]
    model_width = residual.shape[1]
    attended, normed = attention(
        queries, fresh_key_values, cache, lengths, out_weight, residual, norm_gain
    )
    own_live = jnp.arange(slot_rows, dtype=jnp.int32) < lengths[0, 0]
    group_count = lax.axis_size("grp")
    experts = up_gate_weight.shape[0] * group_count * seq_devices
    top_count = expert_ids.shape[1]
    capacity = max(2, 8 * slot_rows * top_count // (5 * experts))
    hidden_width = down_weight.shape[1]
    choose = expert_ids[:, :, None] == jnp.arange(experts, dtype=jnp.int32)[None, None, :]
    routed = (jnp.any(choose, axis=1) & own_live[:, None]).astype(jnp.float32)
    earlier = (jnp.arange(slot_rows)[:, None] > jnp.arange(slot_rows)[None, :]).astype(jnp.float32)
    prefix = jnp.dot(earlier, routed, precision=lax.Precision.HIGHEST)
    slot_in = jnp.sum(jnp.where(choose, prefix[:, None, :], 0.0), axis=2).astype(jnp.int32)
    dump_slot = experts * capacity
    target = jnp.where(own_live[:, None], expert_ids * capacity + slot_in, dump_slot)
    slot_range = jnp.arange(dump_slot, dtype=jnp.int32)
    hits = target.T[:, None, :] == slot_range[None, :, None]
    select = jnp.any(hits, axis=0).astype(jnp.bfloat16)
    outgoing = jnp.dot(select, normed, preferred_element_type=jnp.float32).astype(jnp.bfloat16)
    sectioned = outgoing.reshape(group_count, seq_devices, capacity, model_width)
    arrived = exchange_both(sectioned, ("grp", "sp"), ("grp", "sp"), (0, 1), (0, 1))
    flat_rows = arrived.reshape(-1, model_width)
    projected = jnp.dot(flat_rows, up_gate_weight[0], preferred_element_type=jnp.float32)
    hidden = (jax.nn.silu(projected[:, :hidden_width]) * projected[:, hidden_width:]).astype(
        jnp.bfloat16
    )
    returned = exchange_both(
        jnp.dot(hidden, down_weight[0], preferred_element_type=jnp.float32)
        .astype(jnp.bfloat16)
        .reshape(arrived.shape),
        ("grp", "sp"),
        ("grp", "sp"),
        (0, 1),
        (0, 1),
    )
    matches = target[:, :, None] == slot_range[None, None, :]
    mixing = jnp.sum(jnp.where(matches, gate_values[:, :, None], 0.0), axis=1)
    combined = jnp.dot(
        mixing.astype(jnp.bfloat16),
        returned.reshape(dump_slot, model_width),
        preferred_element_type=jnp.float32,
    )
    moe_out = jnp.where(own_live[:, None], combined, 0.0).astype(jnp.bfloat16)
    return (attended, moe_out)


def solution(mesh):
    in_specs = (
        P(("grp", "sp"), None),
        P(("grp", "sp"), None),
        P("grp", "sp", None, None),
        P("grp", "sp"),
        P("sp", None),
        P(("grp", "sp"), None),
        P(),
        P(("grp", "sp"), None),
        P(("grp", "sp"), None),
        P(("grp", "sp"), None, None),
        P(("grp", "sp"), None, None),
    )
    out_specs = (P(("grp", "sp"), None), P(("grp", "sp"), None))
    return jax.shard_map(
        per_device, mesh=mesh, in_specs=in_specs, out_specs=out_specs, check_vma=False
    )
```

```python
import functools
import math

import jax
import jax.numpy as jnp
from jax import lax
from jax.experimental import pallas as pl
from jax.experimental.pallas import tpu as pltpu
from jax.sharding import PartitionSpec as P


MESH = pl.DeviceIdType.MESH
NEG = -1e30


def group_attention(
    q_hbm, fkv_hbm, cache_hbm, lens_ref, w_hbm, res_hbm, gain_ref,
    attended_ref, normed_ref,
    qb, kx, vx, lb, w, res, heads, own_part, give, take, relay, half_in, full_in,
    q_send, k_send, v_send, l_send, q_recv, k_recv, v_recv, l_recv,
    c_send, c_recv, local, pair_send, pair_recv, ring_send, ring_recv,
):
    me = lax.axis_index("sp")
    devices = qb.shape[0]
    rows, wide = qb.shape[1], qb.shape[2]
    depth = kx.shape[1] // 2
    per = wide // depth
    block = cache_hbm.shape[0]
    cached = 2 * block
    chips = devices // 2
    y, c = me // 2, lax.rem(me, 2)
    partner = y * 2 + 1 - c
    width = w.shape[1]
    half = width // 2

    bar = pltpu.get_barrier_semaphore()
    for i in range(1, devices):
        pl.semaphore_signal(
            bar, inc=1, device_id={"sp": lax.rem(me + i, devices)}, device_id_type=MESH
        )

    local_copies = [
        pltpu.make_async_copy(w_hbm, w, local.at[0]),
        pltpu.make_async_copy(res_hbm, res, local.at[1]),
        pltpu.make_async_copy(
            cache_hbm.at[:, pl.ds(0, depth)],
            kx.at[pl.ds(c * block, block), pl.ds(0, depth)],
            local.at[2],
        ),
        pltpu.make_async_copy(
            cache_hbm.at[:, pl.ds(depth, depth)],
            vx.at[pl.ds(c * block, block), pl.ds(0, depth)],
            local.at[3],
        ),
        pltpu.make_async_copy(
            fkv_hbm.at[:, pl.ds(y * depth, depth)],
            kx.at[pl.ds(cached + me * rows, rows), pl.ds(0, depth)],
            local.at[4],
        ),
        pltpu.make_async_copy(
            fkv_hbm.at[:, pl.ds((chips + y) * depth, depth)],
            vx.at[pl.ds(cached + me * rows, rows), pl.ds(0, depth)],
            local.at[5],
        ),
        pltpu.make_async_copy(q_hbm.at[:, pl.ds(me * wide, wide)], qb.at[me], local.at[6]),
        pltpu.make_async_copy(lens_ref, lb.at[me], local.at[7]),
    ]
    for copy in local_copies:
        copy.start()

    vx[:, depth:] = jnp.ones((vx.shape[0], depth), jnp.bfloat16)
    kx[:cached, depth:] = jnp.zeros((cached, depth), jnp.bfloat16)

    pl.semaphore_wait(bar, devices - 1)

    def k_copy(i):
        p = lax.rem(me + i, devices)
        return pltpu.make_async_remote_copy(
            fkv_hbm.at[:, pl.ds((p // 2) * depth, depth)],
            kx.at[pl.ds(cached + me * rows, rows), pl.ds(0, depth)],
            k_send.at[i], k_recv.at[i], device_id={"sp": p}, device_id_type=MESH,
        )

    def v_copy(i):
        p = lax.rem(me + i, devices)
        return pltpu.make_async_remote_copy(
            fkv_hbm.at[:, pl.ds((chips + p // 2) * depth, depth)],
            vx.at[pl.ds(cached + me * rows, rows), pl.ds(0, depth)],
            v_send.at[i], v_recv.at[i], device_id={"sp": p}, device_id_type=MESH,
        )

    def l_copy(i):
        p = lax.rem(me + i, devices)
        return pltpu.make_async_remote_copy(
            lens_ref, lb.at[me], l_send.at[i], l_recv.at[i],
            device_id={"sp": p}, device_id_type=MESH,
        )

    def q_copy(p):
        return pltpu.make_async_remote_copy(
            q_hbm.at[:, pl.ds(p * wide, wide)], qb.at[me], q_send.at[p], q_recv.at[me],
            device_id={"sp": p}, device_id_type=MESH,
        )

    cache_copies = [
        pltpu.make_async_remote_copy(
            cache_hbm.at[:, pl.ds(d * depth, depth)],
            dst.at[pl.ds(c * block, block), pl.ds(0, depth)],
            c_send.at[d], c_recv.at[d], device_id={"sp": partner}, device_id_type=MESH,
        )
        for d, dst in enumerate((kx, vx))
    ]
    far_first = (4, 5, 3, 2, 6, 1, 7)
    for i in far_first:
        k_copy(i).start()
        v_copy(i).start()
        l_copy(i).start()
    for copy in cache_copies:
        copy.start()
    q_copy(partner).start()
    for dy in (2, 1, 3):
        for cc in range(2):
            q_copy(lax.rem(y + dy, chips) * 2 + cc).start()

    for copy in local_copies:
        copy.wait()
    for copy in cache_copies:
        copy.wait_recv()
    for i in range(1, devices):
        l_copy(i).wait_recv()
        k_copy(i).wait_recv()
        v_copy(i).wait_recv()
    row_ids = lax.broadcasted_iota(jnp.int32, (rows, depth), 0)
    for t in range(devices):
        alive = row_ids < lb[t, 0:1, :]
        kx[cached + t * rows : cached + (t + 1) * rows, depth:] = jnp.where(
            alive, 0.0, NEG
        ).astype(jnp.bfloat16)

    scale = math.log2(math.e) / math.sqrt(depth)
    pair_rows = 2 * rows
    lane = lax.broadcasted_iota(jnp.int32, (pair_rows, depth), 1)
    pick = jnp.where(lane == 0, 1.0, 0.0).astype(jnp.bfloat16)

    def attend(chip):
        keys = cached + (chip + 1) * pair_rows
        first = (cached + chip * pair_rows) // 128 * 128
        shift = cached + chip * pair_rows - first

        def head(h, carry):
            q = qb[2 * chip : 2 * chip + 2, :, pl.ds(pl.multiple_of(h * depth, depth), depth)]
            q = jnp.concatenate([q.reshape(pair_rows, depth), pick], axis=1)
            dims = (((1,), (1,)), ((), ()))
            sa = lax.dot_general(q, kx[:first, :], dims, preferred_element_type=jnp.float32)
            sb = lax.dot_general(q, kx[first:keys, :], dims, preferred_element_type=jnp.float32)
            i = lax.broadcasted_iota(jnp.int32, sb.shape, 0)
            j = lax.broadcasted_iota(jnp.int32, sb.shape, 1)
            sb = jnp.where(j - shift <= i, sb, NEG)
            top = jnp.maximum(
                jnp.max(sa, axis=1, keepdims=True), jnp.max(sb, axis=1, keepdims=True)
            )
            pa = jnp.exp2((sa - top) * scale).astype(jnp.bfloat16)
            pb = jnp.exp2((sb - top) * scale).astype(jnp.bfloat16)
            out = jnp.dot(pa, vx[:first, :], preferred_element_type=jnp.float32)
            out = out + jnp.dot(pb, vx[first:keys, :], preferred_element_type=jnp.float32)
            heads[:, pl.ds(pl.multiple_of(h * depth, depth), depth)] = (
                out[:, :depth] / out[:, depth:]
            ).astype(jnp.bfloat16)
            return carry

        lax.fori_loop(0, per, head, 0)

    def pair_copy(slot):
        return pltpu.make_async_remote_copy(
            give.at[slot], take.at[slot], pair_send.at[slot], pair_recv.at[slot],
            device_id={"sp": partner}, device_id_type=MESH,
        )

    up = lax.rem(y + 1, chips) * 2 + c
    down = lax.rem(y + chips - 1, chips) * 2 + c

    def ring_copy(n):
        src, dst, to = (
            (relay.at[0, :, pl.ds(0, half)], half_in.at[0], up),
            (relay.at[0, :, pl.ds(half, half)], half_in.at[1], down),
            (relay.at[1], full_in.at[0], up),
            (relay.at[2], full_in.at[1], down),
        )[n]
        return pltpu.make_async_remote_copy(
            src, dst, ring_send.at[n], ring_recv.at[n],
            device_id={"sp": to}, device_id_type=MESH,
        )

    def project(side, store):
        mine = heads[pl.ds(pl.multiple_of(side * rows, rows), rows), :]
        for n in range(4):
            cols = slice(n * (width // 4), (n + 1) * (width // 4))
            store(cols, jnp.dot(mine, w[:, cols], preferred_element_type=jnp.float32))

    def step(n, carry):
        dy = jnp.where(n == 3, 3, lax.rem(n * 2, 3))
        chip = lax.rem(y + dy, chips)

        @pl.when(n > 0)
        def _():
            for cc in range(2):
                t = chip * 2 + cc
                pltpu.make_async_copy(qb.at[t], qb.at[t], q_recv.at[t]).wait()

        @pl.when(n == 0)
        def _():
            pltpu.make_async_copy(qb.at[partner], qb.at[partner], q_recv.at[partner]).wait()

        lax.switch(chip, [functools.partial(attend, k) for k in range(chips)])

        def to_give(cols, value):
            give[n, :, cols] = value.astype(jnp.bfloat16)

        def to_own(cols, value):
            own_part[n, :, cols] = value

        project(1 - c, to_give)
        pair_copy(n).start()
        project(c, to_own)

        @pl.when(n == 1)
        def _():
            pair_copy(1).wait_recv()
            relay[0] = (own_part[1] + take[1].astype(jnp.float32)).astype(jnp.bfloat16)
            ring_copy(0).start()
            ring_copy(1).start()

        @pl.when(n == 2)
        def _():
            pair_copy(2).wait_recv()
            ring_copy(0).wait_recv()
            relay[1, :, :half] = (
                own_part[2, :, :half]
                + take[2, :, :half].astype(jnp.float32)
                + half_in[0].astype(jnp.float32)
            ).astype(jnp.bfloat16)
            relay[1, :, half:] = (
                own_part[2, :, half:] + take[2, :, half:].astype(jnp.float32)
            ).astype(jnp.bfloat16)
            ring_copy(2).start()

        @pl.when(n == 3)
        def _():
            pair_copy(3).wait_recv()
            ring_copy(1).wait_recv()
            relay[2, :, :half] = (
                own_part[3, :, :half] + take[3, :, :half].astype(jnp.float32)
            ).astype(jnp.bfloat16)
            relay[2, :, half:] = (
                own_part[3, :, half:]
                + take[3, :, half:].astype(jnp.float32)
                + half_in[1].astype(jnp.float32)
            ).astype(jnp.bfloat16)
            ring_copy(3).start()

        return carry

    lax.fori_loop(0, chips, step, 0)
    pair_copy(0).wait_recv()
    own_part[0] = own_part[0] + take[0].astype(jnp.float32)
    ring_copy(2).wait_recv()
    own_part[0] = own_part[0] + full_in[0].astype(jnp.float32)
    ring_copy(3).wait_recv()
    total = own_part[0] + full_in[1].astype(jnp.float32)
    alive = lax.broadcasted_iota(jnp.int32, (rows, 128), 0) < lens_ref[0:1, :]
    keep = jnp.max(jnp.where(alive, 1.0, 0.0), axis=1, keepdims=True)
    attended_ref[...] = jnp.where(keep > 0.0, total, 0.0).astype(jnp.bfloat16)
    mixed = res[...].astype(jnp.float32) + total
    power = jnp.mean(mixed * mixed, axis=1, keepdims=True)
    normed_ref[...] = (mixed * lax.rsqrt(power + 1e-06) * gain_ref[...]).astype(jnp.bfloat16)

    for i in range(1, devices):
        k_copy(i).wait_send()
        v_copy(i).wait_send()
        l_copy(i).wait_send()
        q_copy(lax.rem(me + i, devices)).wait_send()
    for copy in cache_copies:
        copy.wait_send()
    for n in range(4):
        pair_copy(n).wait_send()
        ring_copy(n).wait_send()


def attention(queries, fresh_key_values, cache, lengths, out_weight, residual, norm_gain):
    devices = lax.axis_size("sp")
    rows, wide = queries.shape[0], queries.shape[1] // devices
    block, depth = cache.shape[2], cache.shape[3] // 2
    width = residual.shape[1]
    keys = 2 * block + devices * rows
    any_spec = pl.BlockSpec(memory_space=pl.ANY)
    vmem = pl.BlockSpec(memory_space=pltpu.VMEM)
    dma = pltpu.SemaphoreType.DMA
    out = jax.ShapeDtypeStruct((rows, width), jnp.bfloat16)
    return pl.pallas_call(
        group_attention,
        out_shape=(out, out),
        in_specs=[any_spec, any_spec, any_spec, vmem, any_spec, any_spec, vmem],
        out_specs=(vmem, vmem),
        scratch_shapes=[
            pltpu.VMEM((devices, rows, wide), jnp.bfloat16),
            pltpu.VMEM((keys, 2 * depth), jnp.bfloat16),
            pltpu.VMEM((keys, 2 * depth), jnp.bfloat16),
            pltpu.VMEM((devices, 8, 128), jnp.int32),
            pltpu.VMEM(out_weight.shape, jnp.bfloat16),
            pltpu.VMEM((rows, width), jnp.bfloat16),
            pltpu.VMEM((2 * rows, wide), jnp.bfloat16),
            pltpu.VMEM((4, rows, width), jnp.float32),
            pltpu.VMEM((4, rows, width), jnp.bfloat16),
            pltpu.VMEM((4, rows, width), jnp.bfloat16),
            pltpu.VMEM((3, rows, width), jnp.bfloat16),
            pltpu.VMEM((2, rows, width // 2), jnp.bfloat16),
            pltpu.VMEM((2, rows, width), jnp.bfloat16),
            dma((devices,)), dma((devices,)), dma((devices,)), dma((devices,)),
            dma((devices,)), dma((devices,)), dma((devices,)), dma((devices,)),
            dma((2,)), dma((2,)), dma((8,)), dma((4,)), dma((4,)), dma((4,)), dma((4,)),
        ],
        compiler_params=pltpu.CompilerParams(
            collective_id=0, has_side_effects=True, vmem_limit_bytes=56 * 1024 * 1024
        ),
    )(
        queries,
        fresh_key_values,
        cache[0, 0],
        jnp.broadcast_to(lengths, (8, 128)),
        out_weight,
        residual,
        norm_gain[None, :],
    )


SLOTS = 16


def expert_exchange(
    line, columns,
    normed_hbm, meta_hbm, up_hbm, down_hbm,
    out_ref,
    xg0, xg1, xg2, meta, sb0, sb1, sb2, recv, ready, rt0, rt1, rt2,
    rs0, rs1, rs2, pb0, pb1, pb2, up, down, hidden,
    w_sem, meta_send, meta_recv, x_send, x_recv, d_send, d_recv,
    r_send, r_recv, s_send, s_recv,
):
    xg, sb, rt, rs, pb = (xg0, xg1, xg2), (sb0, sb1, sb2), (rt0, rt1, rt2), (rs0, rs1, rs2), (pb0, pb1, pb2)
    grp, sp = lax.axis_index("grp"), lax.axis_index("sp")
    pos = (grp // line, sp // 2, lax.rem(grp, line))
    core = lax.rem(sp, 2)
    rows = meta.shape[3]
    plane = 2 * line * line
    ff, width = down.shape

    def wrap(value):
        return lax.rem(value + 2 * line, line)

    def device(p, cc):
        return (p[0] * line + p[2], p[1] * 2 + cc)

    def others(a):
        return (a + 1) % 3, (a + 2) % 3

    def moved(p, a, value):
        p = list(p)
        p[a] = value
        return p

    def source(group, a, p):
        i, j = others(a)
        return wrap(group - p[i] - p[j])

    def cols(a):
        return pl.ds(columns[a][0], columns[a][1])

    bar = pltpu.get_barrier_semaphore()
    peers = [
        (dx, dy, dz, dc)
        for dx in range(line) for dy in range(line) for dz in range(line) for dc in range(2)
        if dx * dy * dz == 0 and (dx, dy, dz, dc) != (0, 0, 0, 0)
    ]
    for dx, dy, dz, dc in peers:
        p = (lax.rem(pos[0] + dx, line), lax.rem(pos[1] + dy, line), lax.rem(pos[2] + dz, line))
        pl.semaphore_signal(
            bar, inc=1, device_id=device(p, lax.rem(core + dc, 2)), device_id_type=MESH
        )
    weights = (
        pltpu.make_async_copy(up_hbm.at[0], up, w_sem.at[0]),
        pltpu.make_async_copy(down_hbm.at[0], down, w_sem.at[1]),
    )
    for copy in weights:
        copy.start()
    for a in range(3):
        pltpu.make_async_copy(meta_hbm, meta.at[a, pos[a]], meta_recv.at[a, pos[a]]).start()
        pltpu.make_async_copy(
            normed_hbm.at[:, cols(a)], xg[a].at[pos[a]], x_recv.at[a, pos[a]]
        ).start()
    pl.semaphore_wait(bar, len(peers))

    def meta_copy(a, k):
        to = device(moved(pos, a, lax.rem(pos[a] + k, line)), core)
        return pltpu.make_async_remote_copy(
            meta_hbm, meta.at[a, pos[a]], meta_send.at[a, k], meta_recv.at[a, pos[a]],
            device_id=to, device_id_type=MESH,
        )

    def x_copy(a, k):
        to = device(moved(pos, a, lax.rem(pos[a] + k, line)), core)
        return pltpu.make_async_remote_copy(
            normed_hbm.at[:, cols(a)], xg[a].at[pos[a]], x_send.at[a, k], x_recv.at[a, pos[a]],
            device_id=to, device_id_type=MESH,
        )

    hops = sorted(range(1, line), key=lambda k: (min(k, line - k), k))
    for k in hops:
        for a in range(3):
            meta_copy(a, k).start()
    for k in hops:
        for a in range(3):
            x_copy(a, k).start()
    for a in range(3):
        for i in range(line):
            pltpu.make_async_copy(meta.at[a, i], meta.at[a, i], meta_recv.at[a, i]).wait()

    shift = line.bit_length() - 1
    q = lax.broadcasted_iota(jnp.int32, (plane, rows), 0)
    q_u = lax.shift_right_logical(q, shift + 1)
    q_v = lax.bitwise_and(lax.shift_right_logical(q, 1), line - 1)
    q_c = lax.bitwise_and(q, 1)
    big = (plane * SLOTS, plane)
    spread = jnp.where(
        lax.shift_right_logical(lax.broadcasted_iota(jnp.int32, big, 0), 4)
        == lax.broadcasted_iota(jnp.int32, big, 1),
        1.0,
        0.0,
    ).astype(jnp.bfloat16)
    slot = (
        lax.bitwise_and(lax.broadcasted_iota(jnp.int32, (plane * SLOTS, rows), 0), SLOTS - 1) + 1
    ).astype(jnp.float32)

    def routing(a, i, gated):
        u, v = others(a)
        where = [None, None, None]
        where[a], where[u], where[v] = pos[a], q_u, q_v
        expert = ((where[0] * line + where[2]) * line + where[1]) * 2 + q_c
        expert = expert.astype(jnp.float32)
        info = meta[a, i]
        place = jnp.zeros((plane, rows), jnp.float32)
        gate = jnp.zeros((plane, rows), jnp.float32)
        for k in range(8):
            match = info[k : k + 1, :] == expert
            place = place + jnp.where(match, info[8 + k : 9 + k, :], 0.0)
            if gated:
                gate = gate + jnp.where(match, info[16 + k : 17 + k, :], 0.0)
        hit = jnp.dot(spread, place.astype(jnp.bfloat16), preferred_element_type=jnp.float32) == slot
        if gated:
            value = jnp.dot(spread, gate.astype(jnp.bfloat16), preferred_element_type=jnp.float32)
        else:
            value = 1.0
        return jnp.where(hit, value, 0.0).astype(jnp.bfloat16)

    steps = [(0, 0)] + sorted(
        [(i, j) for i in range(line) for j in range(line) if (i, j) != (0, 0)],
        key=lambda o: (
            min(o[0], line - o[0]) + min(o[1], line - o[1]),
            sorted((min(o[0], line - o[0]), min(o[1], line - o[1]))),
        ),
    )

    def plane_peer(a, step, dc):
        u, v = others(a)
        p = moved(pos, u, lax.rem(pos[u] + step[0], line))
        p = moved(p, v, lax.rem(pos[v] + step[1], line))
        return p, lax.rem(core + dc, 2)

    def index_in_plane(a, p, cc):
        u, v = others(a)
        return (p[u] * line + p[v]) * 2 + cc

    def spots():
        for step in steps:
            for dc in range(2):
                for a in range(3):
                    yield a, step, dc

    def dispatch(group, carry):
        for a in range(3):
            i = source(group, a, pos)
            pltpu.make_async_copy(xg[a].at[i], xg[a].at[i], x_recv.at[a, i]).wait()
            picked = jnp.dot(
                routing(a, i, False), xg[a][i], preferred_element_type=jnp.float32
            ).astype(jnp.bfloat16)
            sb[a][group] = picked.reshape(plane, SLOTS, columns[a][1])
        for a, step, dc in spots():
            p, cc = plane_peer(a, step, dc)
            d = moved(pos, a, source(group, a, pos))
            src = sb[a].at[group, index_in_plane(a, p, cc)]
            dst = recv.at[group, d[0], d[2], core, :, cols(a)]
            if step == (0, 0) and dc == 0:
                pltpu.make_async_copy(src, dst, d_recv.at[group]).start()
            else:
                pltpu.make_async_remote_copy(
                    src, dst, d_send.at[a, group], d_recv.at[group],
                    device_id=device(p, cc), device_id_type=MESH,
                ).start()
        return carry

    lax.fori_loop(0, line, dispatch, 0)
    for copy in weights:
        copy.wait()

    block = min(256, ff)
    wide = min(512, width)

    def experts(group, carry):
        pltpu.make_async_copy(recv.at[group], recv.at[group], d_recv.at[group]).wait()

        def first(j, inner):
            x = recv[group].reshape(plane * SLOTS, width)
            at = pl.multiple_of(j * block, block)
            gate = jnp.dot(x, up[:, pl.ds(at, block)], preferred_element_type=jnp.float32)
            lift = jnp.dot(x, up[:, pl.ds(ff + at, block)], preferred_element_type=jnp.float32)
            hidden[:, pl.ds(at, block)] = (gate / (1.0 + jnp.exp(-gate)) * lift).astype(jnp.bfloat16)
            return inner

        lax.fori_loop(0, ff // block, first, 0)

        def second(j, inner):
            at = pl.multiple_of(j * wide, wide)
            value = jnp.dot(
                hidden[...], down[:, pl.ds(at, wide)], preferred_element_type=jnp.float32
            )
            ready[group, :, :, :, :, pl.ds(at, wide)] = value.astype(jnp.bfloat16).reshape(
                line, line, 2, SLOTS, wide
            )
            return inner

        lax.fori_loop(0, width // wide, second, 0)
        for a, step, dc in spots():
            p, cc = plane_peer(a, step, dc)
            d = moved(p, a, source(group, a, p))
            src = ready.at[group, d[0], d[2], cc, :, cols(a)]
            dst = rt[a].at[group, index_in_plane(a, pos, core)]
            if step == (0, 0) and dc == 0:
                pltpu.make_async_copy(src, dst, r_recv.at[a, group]).start()
            else:
                pltpu.make_async_remote_copy(
                    src, dst, r_send.at[a, group], r_recv.at[a, group],
                    device_id=device(p, cc), device_id_type=MESH,
                ).start()
        return carry

    lax.fori_loop(0, line, experts, 0)

    def s_copy(a, i):
        to = device(moved(pos, a, i), core)
        return pltpu.make_async_remote_copy(
            pb[a].at[i], rs[a].at[pos[a]], s_send.at[a, i], s_recv.at[a, pos[a]],
            device_id=to, device_id_type=MESH,
        )

    def combine(group, carry):
        for a in range(3):
            i = source(group, a, pos)
            pltpu.make_async_copy(rt[a].at[group], rt[a].at[group], r_recv.at[a, group]).wait()
            share = lax.dot_general(
                routing(a, i, True),
                rt[a][group].reshape(plane * SLOTS, columns[a][1]),
                (((0,), (0,)), ((), ())),
                preferred_element_type=jnp.float32,
            )
            pb[a][i] = share.astype(jnp.bfloat16)

            @pl.when(i != pos[a])
            def _():
                s_copy(a, i).start()

        return carry

    lax.fori_loop(0, line, combine, 0)
    for a in range(3):
        total = pb[a][pos[a]].astype(jnp.float32)
        for k in range(1, line):
            i = lax.rem(pos[a] + k, line)
            pltpu.make_async_copy(rs[a].at[i], rs[a].at[i], s_recv.at[a, i]).wait()
            total = total + rs[a][i].astype(jnp.float32)
        out_ref[:, columns[a][0] : columns[a][0] + columns[a][1]] = total.astype(jnp.bfloat16)

    for a in range(3):
        for k in range(1, line):
            meta_copy(a, k).wait_send()
            x_copy(a, k).wait_send()
            s_copy(a, lax.rem(pos[a] + k, line)).wait_send()
        for group in range(line):
            sent = sb[a].at[group, pl.ds(0, plane - 1)]
            pltpu.make_async_copy(sent, sent, d_send.at[a, group]).wait()
            back = rt[a].at[group, pl.ds(0, plane - 1)]
            pltpu.make_async_copy(back, back, r_send.at[a, group]).wait()


def mix_experts(normed, meta, up_gate_weight, down_weight):
    line = math.isqrt(lax.axis_size("grp"))
    rows, width = normed.shape
    ff = down_weight.shape[1]
    plane = 2 * line * line
    tiles = width // 128
    cuts = [0, tiles // 3, 2 * (tiles // 3), tiles]
    columns = [(128 * cuts[a], 128 * (cuts[a + 1] - cuts[a])) for a in range(3)]
    any_spec = pl.BlockSpec(memory_space=pl.ANY)
    dma = pltpu.SemaphoreType.DMA

    def buffers(*shape):
        return [pltpu.VMEM((*shape, columns[a][1]), jnp.bfloat16) for a in range(3)]

    whole = pltpu.VMEM((line, line, line, 2, SLOTS, width), jnp.bfloat16)
    return pl.pallas_call(
        functools.partial(expert_exchange, line, columns),
        out_shape=jax.ShapeDtypeStruct((rows, width), jnp.bfloat16),
        in_specs=[any_spec] * 4,
        out_specs=pl.BlockSpec(memory_space=pltpu.VMEM),
        scratch_shapes=[
            *buffers(line, rows),
            pltpu.VMEM((3, line, *meta.shape), jnp.float32),
            *buffers(line, plane, SLOTS),
            whole,
            whole,
            *buffers(line, plane, SLOTS),
            *buffers(line, rows),
            *buffers(line, rows),
            pltpu.VMEM(up_gate_weight.shape[1:], jnp.bfloat16),
            pltpu.VMEM(down_weight.shape[1:], jnp.bfloat16),
            pltpu.VMEM((plane * SLOTS, ff), jnp.bfloat16),
            dma((2,)),
            dma((3, line)), dma((3, line)), dma((3, line)), dma((3, line)),
            dma((3, line)), dma((line,)), dma((3, line)), dma((3, line)),
            dma((3, line)), dma((3, line)),
        ],
        compiler_params=pltpu.CompilerParams(
            collective_id=1, has_side_effects=True, vmem_limit_bytes=67_000_000
        ),
    )(normed, meta, up_gate_weight, down_weight)


def per_device(
    queries,
    fresh_key_values,
    cache,
    lengths,
    out_weight,
    residual,
    norm_gain,
    expert_ids,
    gate_values,
    up_gate_weight,
    down_weight,
):
    seq_devices = lax.axis_size("sp")
    slot_rows = queries.shape[0]
    attended, normed = attention(
        queries, fresh_key_values, cache, lengths, out_weight, residual, norm_gain
    )
    own_live = jnp.arange(slot_rows, dtype=jnp.int32) < lengths[0, 0]
    experts = up_gate_weight.shape[0] * lax.axis_size("grp") * lax.axis_size("sp")
    choose = expert_ids[:, :, None] == jnp.arange(experts, dtype=jnp.int32)[None, None, :]
    routed = (jnp.any(choose, axis=1) & own_live[:, None]).astype(jnp.float32)
    earlier = (jnp.arange(slot_rows)[:, None] > jnp.arange(slot_rows)[None, :]).astype(jnp.float32)
    prefix = jnp.dot(earlier, routed, precision=lax.Precision.HIGHEST)
    slot_in = jnp.sum(jnp.where(choose, prefix[:, None, :], 0.0), axis=2)
    chosen = jnp.where(own_live[:, None], expert_ids, experts).astype(jnp.float32)
    meta = jnp.concatenate([chosen, slot_in + 1.0, gate_values], axis=1).T
    return (attended, mix_experts(normed, meta, up_gate_weight, down_weight))


def solution(mesh):
    in_specs = (
        P(("grp", "sp"), None),
        P(("grp", "sp"), None),
        P("grp", "sp", None, None),
        P("grp", "sp"),
        P("sp", None),
        P(("grp", "sp"), None),
        P(),
        P(("grp", "sp"), None),
        P(("grp", "sp"), None),
        P(("grp", "sp"), None, None),
        P(("grp", "sp"), None, None),
    )
    out_specs = (P(("grp", "sp"), None), P(("grp", "sp"), None))
    return jax.shard_map(
        per_device, mesh=mesh, in_specs=in_specs, out_specs=out_specs, check_vma=False
    )
```

```python
import functools
import math

import jax
import jax.numpy as jnp
from jax import lax
from jax.experimental import pallas as pl
from jax.experimental.pallas import tpu as pltpu
from jax.sharding import PartitionSpec as P

MESH = pl.DeviceIdType.MESH
NEG = -1e30
SLOTS = 16


def layer(
    line, columns,
    q_hbm, fkv_hbm, cache_hbm, lens_ref, w_hbm, res_hbm, gain_ref, ids_ref, gates_ref, up_hbm, down_hbm,
    attn_ref, moe_ref,
    qb, kx, vx, lb, w, res, heads, own, mine, parts, normed, info,
    xg, meta, sb, recv, rt, rs, pb, up, down, hidden,
    q_send, k_send, v_send, l_send, q_recv, k_recv, v_recv, l_recv,
    c_send, c_recv, local, pair_send, pair_recv, part_send, part_recv,
    w_sem, meta_send, meta_recv, x_send, x_recv, d_send, d_recv,
    r_send, r_recv, s_send, s_recv,
):
    grp, me = lax.axis_index("grp"), lax.axis_index("sp")
    pos = (grp // line, me // 2, lax.rem(grp, line))
    core = lax.rem(me, 2)
    devices, chips = 2 * line, line
    rows, wide = qb.shape[1], qb.shape[2]
    depth = kx.shape[1] // 2
    per = wide // depth
    block = cache_hbm.shape[0]
    cached = 2 * block
    y, c = pos[1], core
    partner = y * 2 + 1 - c
    plane = 2 * line * line
    ff, width = down.shape
    tiles = rows // SLOTS

    def wrap(value):
        return lax.rem(value + 2 * line, line)

    def device(p, cc):
        return (p[0] * line + p[2], p[1] * 2 + cc)

    def others(a):
        return (a + 1) % 3, (a + 2) % 3

    def moved(p, a, value):
        p = list(p)
        p[a] = value
        return p

    def source(group, a, p):
        i, j = others(a)
        return wrap(group - p[i] - p[j])

    def cols(a):
        return pl.ds(columns[a][0], columns[a][1])

    def span(a):
        return slice(columns[a][0], columns[a][0] + columns[a][1])

    bar = pltpu.get_barrier_semaphore()
    peers = [
        (dx, dy, dz, dc)
        for dx in range(line) for dy in range(line) for dz in range(line) for dc in range(2)
        if dx * dy * dz == 0 and (dx, dy, dz, dc) != (0, 0, 0, 0)
    ]
    for dx, dy, dz, dc in peers:
        p = (lax.rem(pos[0] + dx, line), lax.rem(pos[1] + dy, line), lax.rem(pos[2] + dz, line))
        pl.semaphore_signal(
            bar, inc=1, device_id=device(p, lax.rem(core + dc, 2)), device_id_type=MESH
        )

    pltpu.make_async_copy(q_hbm.at[:, pl.ds(me * wide, wide)], qb.at[me], q_recv.at[me]).start()
    local_copies = [
        pltpu.make_async_copy(w_hbm, w, local.at[0]),
        pltpu.make_async_copy(res_hbm, res, local.at[1]),
        pltpu.make_async_copy(
            cache_hbm.at[:, pl.ds(0, depth)],
            kx.at[pl.ds(c * block, block), pl.ds(0, depth)],
            local.at[2],
        ),
        pltpu.make_async_copy(
            cache_hbm.at[:, pl.ds(depth, depth)],
            vx.at[pl.ds(c * block, block), pl.ds(0, depth)],
            local.at[3],
        ),
        pltpu.make_async_copy(
            fkv_hbm.at[:, pl.ds(y * depth, depth)],
            kx.at[pl.ds(cached + me * rows, rows), pl.ds(0, depth)],
            local.at[4],
        ),
        pltpu.make_async_copy(
            fkv_hbm.at[:, pl.ds((chips + y) * depth, depth)],
            vx.at[pl.ds(cached + me * rows, rows), pl.ds(0, depth)],
            local.at[5],
        ),
        pltpu.make_async_copy(lens_ref, lb.at[me], local.at[6]),
    ]
    for copy in local_copies:
        copy.start()
    weights = (
        pltpu.make_async_copy(up_hbm.at[0], up, w_sem.at[0]),
        pltpu.make_async_copy(down_hbm.at[0], down, w_sem.at[1]),
    )
    vx[:, depth:] = jnp.ones((vx.shape[0], depth), jnp.bfloat16)
    kx[:cached, depth:] = jnp.zeros((cached, depth), jnp.bfloat16)

    pl.semaphore_wait(bar, len(peers))

    def k_copy(i):
        p = lax.rem(me + i, devices)
        return pltpu.make_async_remote_copy(
            fkv_hbm.at[:, pl.ds((p // 2) * depth, depth)],
            kx.at[pl.ds(cached + me * rows, rows), pl.ds(0, depth)],
            k_send.at[i], k_recv.at[me], device_id={"sp": p}, device_id_type=MESH,
        )

    def v_copy(i):
        p = lax.rem(me + i, devices)
        return pltpu.make_async_remote_copy(
            fkv_hbm.at[:, pl.ds((chips + p // 2) * depth, depth)],
            vx.at[pl.ds(cached + me * rows, rows), pl.ds(0, depth)],
            v_send.at[i], v_recv.at[me], device_id={"sp": p}, device_id_type=MESH,
        )

    def l_copy(i):
        p = lax.rem(me + i, devices)
        return pltpu.make_async_remote_copy(
            lens_ref, lb.at[me], l_send.at[i], l_recv.at[me],
            device_id={"sp": p}, device_id_type=MESH,
        )

    def q_copy(i):
        p = lax.rem(me + i, devices)
        return pltpu.make_async_remote_copy(
            q_hbm.at[:, pl.ds(p * wide, wide)], qb.at[me], q_send.at[i], q_recv.at[me],
            device_id={"sp": p}, device_id_type=MESH,
        )

    cache_copies = [
        pltpu.make_async_remote_copy(
            cache_hbm.at[:, pl.ds(d * depth, depth)],
            dst.at[pl.ds(c * block, block), pl.ds(0, depth)],
            c_send.at[d], c_recv.at[d], device_id={"sp": partner}, device_id_type=MESH,
        )
        for d, dst in enumerate((kx, vx))
    ]
    far_first = sorted(range(1, devices), key=lambda i: -min(i, devices - i))
    for i in far_first:
        k_copy(i).start()
        v_copy(i).start()
        l_copy(i).start()
    for copy in cache_copies:
        copy.start()
    for i in far_first:
        q_copy(i).start()
    for copy in weights:
        copy.start()

    experts = plane * line
    lanes = lax.broadcasted_iota(jnp.int32, (8, rows), 1)
    living = lanes < lens_ref[:, 0:1]
    expert_rows = lax.broadcasted_iota(jnp.int32, (experts, rows), 0)
    named = jnp.where(living, ids_ref[...], experts)
    routed = jnp.zeros((experts, rows), jnp.float32)
    for k in range(8):
        routed = routed + jnp.where(named[k : k + 1, :] == expert_rows, 1.0, 0.0)
    square = (rows, rows)
    before = jnp.where(
        lax.broadcasted_iota(jnp.int32, square, 0) < lax.broadcasted_iota(jnp.int32, square, 1),
        1.0,
        0.0,
    ).astype(jnp.bfloat16)
    prefix = jnp.dot(routed.astype(jnp.bfloat16), before, preferred_element_type=jnp.float32)
    info[0:8, :] = named.astype(jnp.float32)
    for k in range(8):
        hits = jnp.where(named[k : k + 1, :] == expert_rows, prefix, 0.0)
        info[8 + k : 9 + k, :] = jnp.sum(hits, axis=0, keepdims=True) + 1.0
    info[16:24, :] = gates_ref[...]

    for copy in local_copies:
        copy.wait()
    for copy in cache_copies:
        copy.wait_recv()
    row_ids = lax.broadcasted_iota(jnp.int32, (rows, depth), 0)
    for i in range(1, devices):
        t = lax.rem(me + i, devices)
        at = pl.ds(cached + t * rows, rows)
        left = pl.ds(0, depth)
        pltpu.make_async_copy(lb.at[t], lb.at[t], l_recv.at[t]).wait()
        pltpu.make_async_copy(kx.at[at, left], kx.at[at, left], k_recv.at[t]).wait()
        pltpu.make_async_copy(vx.at[at, left], vx.at[at, left], v_recv.at[t]).wait()
    for t in range(devices):
        alive = row_ids < lb[t, 0:1, :]
        kx[cached + t * rows : cached + (t + 1) * rows, depth:] = jnp.where(
            alive, 0.0, NEG
        ).astype(jnp.bfloat16)

    def meta_copy(a, k):
        to = device(moved(pos, a, lax.rem(pos[a] + k, line)), core)
        return pltpu.make_async_remote_copy(
            info, meta.at[a, pos[a]], meta_send.at[a, k], meta_recv.at[a, pos[a]],
            device_id=to, device_id_type=MESH,
        )

    for a in range(3):
        pltpu.make_async_copy(info, meta.at[a, pos[a]], meta_recv.at[a, pos[a]]).start()
        for k in range(1, line):
            meta_copy(a, k).start()

    scale = math.log2(math.e) / math.sqrt(depth)
    pair_rows = 2 * rows
    lane = lax.broadcasted_iota(jnp.int32, (pair_rows, depth), 1)
    pick = jnp.where(lane == 0, 1.0, 0.0).astype(jnp.bfloat16)

    def attend(chip):
        keys = cached + (chip + 1) * pair_rows
        first = (cached + chip * pair_rows) // 128 * 128
        shift = cached + chip * pair_rows - first

        def head(h, carry):
            q = qb[2 * chip : 2 * chip + 2, :, pl.ds(pl.multiple_of(h * depth, depth), depth)]
            q = jnp.concatenate([q.reshape(pair_rows, depth), pick], axis=1)
            dims = (((1,), (1,)), ((), ()))
            sa = lax.dot_general(q, kx[:first, :], dims, preferred_element_type=jnp.float32)
            sb = lax.dot_general(q, kx[first:keys, :], dims, preferred_element_type=jnp.float32)
            i = lax.broadcasted_iota(jnp.int32, sb.shape, 0)
            j = lax.broadcasted_iota(jnp.int32, sb.shape, 1)
            sb = jnp.where(j - shift <= i, sb, NEG)
            top = jnp.maximum(
                jnp.max(sa, axis=1, keepdims=True), jnp.max(sb, axis=1, keepdims=True)
            )
            pa = jnp.exp2((sa - top) * scale).astype(jnp.bfloat16)
            pb = jnp.exp2((sb - top) * scale).astype(jnp.bfloat16)
            out = jnp.dot(pa, vx[:first, :], preferred_element_type=jnp.float32)
            out = out + jnp.dot(pb, vx[first:keys, :], preferred_element_type=jnp.float32)
            heads[:, pl.ds(pl.multiple_of(h * depth, depth), depth)] = (
                out[:, :depth] / out[:, depth:]
            ).astype(jnp.bfloat16)
            return carry

        lax.fori_loop(0, per, head, 0)

    def pair_copy(n):
        return pltpu.make_async_remote_copy(
            rt.at[n, pl.ds(0, tiles)], rt.at[n, pl.ds(tiles, tiles)], pair_send.at[n], pair_recv.at[n],
            device_id={"sp": partner}, device_id_type=MESH,
        )

    def goal(n):
        return wrap(n - pos[0] - pos[2])

    def part_copy(n):
        ahead = wrap(goal(n) - y)
        return pltpu.make_async_remote_copy(
            rt.at[n, pl.ds(2 * tiles, tiles)], parts.at[ahead - 1], part_send.at[n], part_recv.at[ahead - 1],
            device_id={"sp": goal(n) * 2 + c}, device_id_type=MESH,
        )

    wide_cols = min(512, width)

    def project(side, store):
        some = heads[pl.ds(pl.multiple_of(side * rows, rows), rows), :]
        for n in range(0, width, wide_cols):
            part = slice(n, min(width, n + wide_cols))
            store(part, jnp.dot(some, w[:, part], preferred_element_type=jnp.float32))

    def step(n, carry):
        chip = goal(n)
        for cc in range(2):
            t = chip * 2 + cc
            pltpu.make_async_copy(qb.at[t], qb.at[t], q_recv.at[t]).wait()
        lax.switch(chip, [functools.partial(attend, k) for k in range(chips)])

        def to_give(part, value):
            rt[n, 0:tiles, :, part] = value.astype(jnp.bfloat16).reshape(tiles, SLOTS, value.shape[1])

        def to_own(part, value):
            own[:, part] = value

        project(1 - c, to_give)
        pair_copy(n).start()
        project(c, to_own)
        pair_copy(n).wait_recv()
        both = own[...] + rt[n, tiles : 2 * tiles].reshape(rows, width).astype(jnp.float32)

        @pl.when(chip != y)
        def _():
            rt[n, 2 * tiles : 3 * tiles] = both.astype(jnp.bfloat16).reshape(tiles, SLOTS, width)
            part_copy(n).start()

        @pl.when(chip == y)
        def _():
            mine[...] = both

        return carry

    lax.fori_loop(0, chips, step, 0)

    def x_copy(a, k):
        to = device(moved(pos, a, lax.rem(pos[a] + k, line)), core)
        return pltpu.make_async_remote_copy(
            normed.at[:, cols(a)], xg.at[pos[a], :, cols(a)], x_send.at[a, k], x_recv.at[a, pos[a]],
            device_id=to, device_id_type=MESH,
        )

    hops = sorted(range(1, line), key=lambda k: (-min(k, line - k), k))

    def finish():
        total = mine[...]
        for i in range(line - 1):
            pltpu.make_async_copy(parts.at[i], parts.at[i], part_recv.at[i]).wait()
            total = total + parts[i].reshape(rows, width).astype(jnp.float32)
        attn_ref[...] = total.astype(jnp.bfloat16)
        mixed = res[...].astype(jnp.float32) + total
        power = jnp.mean(mixed * mixed, axis=1, keepdims=True)
        normed[...] = (mixed * lax.rsqrt(power + 1e-06) * gain_ref[...]).astype(jnp.bfloat16)
        for k in hops:
            for a in range(3):
                x_copy(a, k).start()
        for a in range(3):
            pltpu.make_async_copy(
                normed.at[:, cols(a)], xg.at[pos[a], :, cols(a)], x_recv.at[a, pos[a]]
            ).start()

    for a in range(3):
        for i in range(line):
            pltpu.make_async_copy(meta.at[a, i], meta.at[a, i], meta_recv.at[a, i]).wait()

    shift = line.bit_length() - 1
    q = lax.broadcasted_iota(jnp.int32, (plane, rows), 0)
    q_u = lax.shift_right_logical(q, shift + 1)
    q_v = lax.bitwise_and(lax.shift_right_logical(q, 1), line - 1)
    q_c = lax.bitwise_and(q, 1)
    big = (plane * SLOTS, plane)
    spread = jnp.where(
        lax.shift_right_logical(lax.broadcasted_iota(jnp.int32, big, 0), 4)
        == lax.broadcasted_iota(jnp.int32, big, 1),
        1.0,
        0.0,
    ).astype(jnp.bfloat16)
    slot = (
        lax.bitwise_and(lax.broadcasted_iota(jnp.int32, (plane * SLOTS, rows), 0), SLOTS - 1) + 1
    ).astype(jnp.float32)

    def routing(a, i, gated):
        u, v = others(a)
        where = [None, None, None]
        where[a], where[u], where[v] = pos[a], q_u, q_v
        expert = ((where[0] * line + where[2]) * line + where[1]) * 2 + q_c
        expert = expert.astype(jnp.float32)
        info = meta[a, i]
        place = jnp.zeros((plane, rows), jnp.float32)
        gate = jnp.zeros((plane, rows), jnp.float32)
        for k in range(8):
            match = info[k : k + 1, :] == expert
            place = place + jnp.where(match, info[8 + k : 9 + k, :], 0.0)
            if gated:
                gate = gate + jnp.where(match, info[16 + k : 17 + k, :], 0.0)
        hit = jnp.dot(spread, place.astype(jnp.bfloat16), preferred_element_type=jnp.float32) == slot
        if gated:
            value = jnp.dot(spread, gate.astype(jnp.bfloat16), preferred_element_type=jnp.float32)
        else:
            value = 1.0
        return jnp.where(hit, value, 0.0).astype(jnp.bfloat16)

    steps = [(0, 0)] + sorted(
        [(i, j) for i in range(line) for j in range(line) if (i, j) != (0, 0)],
        key=lambda o: (
            min(o[0], line - o[0]) + min(o[1], line - o[1]),
            sorted((min(o[0], line - o[0]), min(o[1], line - o[1]))),
        ),
    )

    def plane_peer(a, step, dc):
        u, v = others(a)
        p = moved(pos, u, lax.rem(pos[u] + step[0], line))
        p = moved(p, v, lax.rem(pos[v] + step[1], line))
        return p, lax.rem(core + dc, 2)

    def index_in_plane(a, p, cc):
        u, v = others(a)
        return (p[u] * line + p[v]) * 2 + cc

    def spots():
        for step in steps:
            for dc in range(2):
                for a in range(3):
                    yield a, step, dc

    group_mine = lax.rem(pos[0] + pos[1] + pos[2], line)

    def dispatch(group, carry):
        pl.when(group == group_mine)(finish)
        pair_copy(group).wait_send()

        @pl.when(goal(group) != y)
        def _():
            part_copy(group).wait_send()

        for a in range(3):
            i = source(group, a, pos)
            pltpu.make_async_copy(
                xg.at[i, :, cols(a)], xg.at[i, :, cols(a)], x_recv.at[a, i]
            ).wait()
            picked = jnp.dot(
                routing(a, i, False), xg[i, :, span(a)], preferred_element_type=jnp.float32
            ).astype(jnp.bfloat16)
            sb[group, :, :, span(a)] = picked.reshape(plane, SLOTS, columns[a][1])
        for a, step, dc in spots():
            p, cc = plane_peer(a, step, dc)
            d = moved(pos, a, source(group, a, pos))
            src = sb.at[group, index_in_plane(a, p, cc), :, cols(a)]
            dst = recv.at[group, d[0], d[2], core, :, cols(a)]
            if step == (0, 0) and dc == 0:
                pltpu.make_async_copy(src, dst, d_recv.at[group]).start()
            else:
                pltpu.make_async_remote_copy(
                    src, dst, d_send.at[a, group], d_recv.at[group],
                    device_id=device(p, cc), device_id_type=MESH,
                ).start()
        return carry

    lax.fori_loop(0, line, dispatch, 0)
    for copy in weights:
        copy.wait()

    block_ff = min(256, ff)

    def run_experts(group, carry):
        pltpu.make_async_copy(recv.at[group], recv.at[group], d_recv.at[group]).wait()

        def first(j, inner):
            x = recv[group].reshape(plane * SLOTS, width)
            at = pl.multiple_of(j * block_ff, block_ff)
            gate = jnp.dot(x, up[:, pl.ds(at, block_ff)], preferred_element_type=jnp.float32)
            lift = jnp.dot(x, up[:, pl.ds(ff + at, block_ff)], preferred_element_type=jnp.float32)
            hidden[:, pl.ds(at, block_ff)] = (
                gate / (1.0 + jnp.exp(-gate)) * lift
            ).astype(jnp.bfloat16)
            return inner

        lax.fori_loop(0, ff // block_ff, first, 0)

        def second(j, inner):
            at = pl.multiple_of(j * wide_cols, wide_cols)
            value = jnp.dot(
                hidden[...], down[:, pl.ds(at, wide_cols)], preferred_element_type=jnp.float32
            )
            recv[group, :, :, :, :, pl.ds(at, wide_cols)] = value.astype(jnp.bfloat16).reshape(
                line, line, 2, SLOTS, wide_cols
            )
            return inner

        lax.fori_loop(0, width // wide_cols, second, 0)
        for a, step, dc in spots():
            p, cc = plane_peer(a, step, dc)
            d = moved(p, a, source(group, a, p))
            src = recv.at[group, d[0], d[2], cc, :, cols(a)]
            dst = rt.at[group, index_in_plane(a, pos, core), :, cols(a)]
            if step == (0, 0) and dc == 0:
                pltpu.make_async_copy(src, dst, r_recv.at[a, group]).start()
            else:
                pltpu.make_async_remote_copy(
                    src, dst, r_send.at[a, group], r_recv.at[a, group],
                    device_id=device(p, cc), device_id_type=MESH,
                ).start()
        return carry

    lax.fori_loop(0, line, run_experts, 0)

    def s_copy(a, i):
        to = device(moved(pos, a, i), core)
        return pltpu.make_async_remote_copy(
            pb.at[i, :, cols(a)], rs.at[pos[a], :, cols(a)], s_send.at[a, i], s_recv.at[a, pos[a]],
            device_id=to, device_id_type=MESH,
        )

    def combine(group, carry):
        for a in range(3):
            i = source(group, a, pos)
            landed = rt.at[group, :, :, cols(a)]
            pltpu.make_async_copy(landed, landed, r_recv.at[a, group]).wait()
            share = lax.dot_general(
                routing(a, i, True),
                rt[group, :, :, span(a)].reshape(plane * SLOTS, columns[a][1]),
                (((0,), (0,)), ((), ())),
                preferred_element_type=jnp.float32,
            )
            pb[i, :, span(a)] = share.astype(jnp.bfloat16)

            @pl.when(i != pos[a])
            def _():
                s_copy(a, i).start()

        return carry

    lax.fori_loop(0, line, combine, 0)
    for a in range(3):
        total = pb[pos[a], :, span(a)].astype(jnp.float32)
        for k in range(1, line):
            i = lax.rem(pos[a] + k, line)
            landed = rs.at[i, :, cols(a)]
            pltpu.make_async_copy(landed, landed, s_recv.at[a, i]).wait()
            total = total + rs[i, :, span(a)].astype(jnp.float32)
        moe_ref[:, span(a)] = total.astype(jnp.bfloat16)

    for i in range(1, devices):
        k_copy(i).wait_send()
        v_copy(i).wait_send()
        l_copy(i).wait_send()
        q_copy(i).wait_send()
    for copy in cache_copies:
        copy.wait_send()
    for a in range(3):
        for k in range(1, line):
            meta_copy(a, k).wait_send()
            x_copy(a, k).wait_send()
            s_copy(a, lax.rem(pos[a] + k, line)).wait_send()
        for group in range(line):
            sent = sb.at[group, pl.ds(0, plane - 1), :, cols(a)]
            pltpu.make_async_copy(sent, sent, d_send.at[a, group]).wait()
            pltpu.make_async_copy(sent, sent, r_send.at[a, group]).wait()


def per_device(
    queries,
    fresh_key_values,
    cache,
    lengths,
    out_weight,
    residual,
    norm_gain,
    expert_ids,
    gate_values,
    up_gate_weight,
    down_weight,
):
    devices = lax.axis_size("sp")
    line = devices // 2
    rows, wide = queries.shape[0], queries.shape[1] // devices
    block, depth = cache.shape[2], cache.shape[3] // 2
    width, ff = residual.shape[1], down_weight.shape[1]
    keys = 2 * block + devices * rows
    plane = 2 * line * line
    share = width // 128
    narrow = share // 3
    cuts = [0, narrow, share - narrow, share]
    columns = [(128 * cuts[a], 128 * (cuts[a + 1] - cuts[a])) for a in range(3)]
    any_spec = pl.BlockSpec(memory_space=pl.ANY)
    vmem = pl.BlockSpec(memory_space=pltpu.VMEM)
    dma = pltpu.SemaphoreType.DMA
    half = jnp.bfloat16
    out = jax.ShapeDtypeStruct((rows, width), half)
    top = expert_ids.shape[1]
    attn_sum, mixed = pl.pallas_call(
        functools.partial(layer, line, columns),
        out_shape=(out, out),
        in_specs=[
            any_spec, any_spec, any_spec, vmem, any_spec, any_spec, vmem, vmem, vmem, any_spec, any_spec,
        ],
        out_specs=(vmem, vmem),
        scratch_shapes=[
            pltpu.VMEM((devices, rows, wide), half),
            pltpu.VMEM((keys, 2 * depth), half),
            pltpu.VMEM((keys, 2 * depth), half),
            pltpu.VMEM((devices, 8, 128), jnp.int32),
            pltpu.VMEM(out_weight.shape, half),
            pltpu.VMEM((rows, width), half),
            pltpu.VMEM((2 * rows, wide), half),
            pltpu.VMEM((rows, width), jnp.float32),
            pltpu.VMEM((rows, width), jnp.float32),
            pltpu.VMEM((line - 1, rows // SLOTS, SLOTS, width), half),
            pltpu.VMEM((rows, width), half),
            pltpu.VMEM((3 * top, rows), jnp.float32),
            pltpu.VMEM((line, rows, width), half),
            pltpu.VMEM((3, line, 3 * top, rows), jnp.float32),
            pltpu.VMEM((line, plane, SLOTS, width), half),
            pltpu.VMEM((line, line, line, 2, SLOTS, width), half),
            pltpu.VMEM((line, plane, SLOTS, width), half),
            pltpu.VMEM((line, rows, width), half),
            pltpu.VMEM((line, rows, width), half),
            pltpu.VMEM(up_gate_weight.shape[1:], half),
            pltpu.VMEM(down_weight.shape[1:], half),
            pltpu.VMEM((plane * SLOTS, ff), half),
            dma((devices,)), dma((devices,)), dma((devices,)), dma((devices,)),
            dma((devices,)), dma((devices,)), dma((devices,)), dma((devices,)),
            dma((2,)), dma((2,)), dma((7,)), dma((line,)), dma((line,)), dma((line,)), dma((line,)),
            dma((2,)),
            dma((3, line)), dma((3, line)), dma((3, line)), dma((3, line)),
            dma((3, line)), dma((line,)), dma((3, line)), dma((3, line)),
            dma((3, line)), dma((3, line)),
        ],
        compiler_params=pltpu.CompilerParams(
            collective_id=0, has_side_effects=True, vmem_limit_bytes=67_000_000
        ),
    )(
        queries,
        fresh_key_values,
        cache[0, 0],
        jnp.broadcast_to(lengths, (8, 128)),
        out_weight,
        residual,
        norm_gain[None, :],
        expert_ids.T,
        gate_values.T,
        up_gate_weight,
        down_weight,
    )
    own_live = (jnp.arange(rows, dtype=jnp.int32) < lengths[0, 0])[:, None]
    zero = jnp.zeros((), half)
    return (jnp.where(own_live, attn_sum, zero), jnp.where(own_live, mixed, zero))


def solution(mesh):
    in_specs = (
        P(("grp", "sp"), None),
        P(("grp", "sp"), None),
        P("grp", "sp", None, None),
        P("grp", "sp"),
        P("sp", None),
        P(("grp", "sp"), None),
        P(),
        P(("grp", "sp"), None),
        P(("grp", "sp"), None),
        P(("grp", "sp"), None, None),
        P(("grp", "sp"), None, None),
    )
    out_specs = (P(("grp", "sp"), None), P(("grp", "sp"), None))
    return jax.shard_map(
        per_device, mesh=mesh, in_specs=in_specs, out_specs=out_specs, check_vma=False
    )
```

```python
import functools
import math

import jax
import jax.numpy as jnp
from jax import lax
from jax.experimental import pallas as pl
from jax.experimental.pallas import tpu as pltpu
from jax.sharding import PartitionSpec as P


MESH = pl.DeviceIdType.MESH
NEG = -1e30


def group_attention(
    experts,
    q_hbm, fkv_hbm, cache_hbm, lens_ref, w_hbm, res_hbm, gain_ref, ids_ref, gates_ref,
    attended_ref, normed_ref, info,
    qb, kx, vx, lb, w, res, heads, own_part, give, take, relay, half_in, full_in,
    q_send, k_send, v_send, l_send, q_recv, k_recv, v_recv, l_recv,
    c_send, c_recv, local, pair_send, pair_recv, ring_send, ring_recv,
):
    me = lax.axis_index("sp")
    devices = qb.shape[0]
    rows, wide = qb.shape[1], qb.shape[2]
    depth = kx.shape[1] // 2
    per = wide // depth
    block = cache_hbm.shape[0]
    cached = 2 * block
    chips = devices // 2
    y, c = me // 2, lax.rem(me, 2)
    partner = y * 2 + 1 - c
    width = w.shape[1]
    half = width // 2

    bar = pltpu.get_barrier_semaphore()
    for i in range(1, devices):
        pl.semaphore_signal(
            bar, inc=1, device_id={"sp": lax.rem(me + i, devices)}, device_id_type=MESH
        )

    local_copies = [
        pltpu.make_async_copy(w_hbm, w, local.at[0]),
        pltpu.make_async_copy(res_hbm, res, local.at[1]),
        pltpu.make_async_copy(
            cache_hbm.at[:, pl.ds(0, depth)],
            kx.at[pl.ds(c * block, block), pl.ds(0, depth)],
            local.at[2],
        ),
        pltpu.make_async_copy(
            cache_hbm.at[:, pl.ds(depth, depth)],
            vx.at[pl.ds(c * block, block), pl.ds(0, depth)],
            local.at[3],
        ),
        pltpu.make_async_copy(
            fkv_hbm.at[:, pl.ds(y * depth, depth)],
            kx.at[pl.ds(cached + me * rows, rows), pl.ds(0, depth)],
            local.at[4],
        ),
        pltpu.make_async_copy(
            fkv_hbm.at[:, pl.ds((chips + y) * depth, depth)],
            vx.at[pl.ds(cached + me * rows, rows), pl.ds(0, depth)],
            local.at[5],
        ),
        pltpu.make_async_copy(q_hbm.at[:, pl.ds(me * wide, wide)], qb.at[me], local.at[6]),
        pltpu.make_async_copy(lens_ref, lb.at[me], local.at[7]),
    ]
    for copy in local_copies:
        copy.start()

    vx[:, depth:] = jnp.ones((vx.shape[0], depth), jnp.bfloat16)
    kx[:cached, depth:] = jnp.zeros((cached, depth), jnp.bfloat16)

    pl.semaphore_wait(bar, devices - 1)

    def k_copy(i):
        p = lax.rem(me + i, devices)
        return pltpu.make_async_remote_copy(
            fkv_hbm.at[:, pl.ds((p // 2) * depth, depth)],
            kx.at[pl.ds(cached + me * rows, rows), pl.ds(0, depth)],
            k_send.at[i], k_recv.at[i], device_id={"sp": p}, device_id_type=MESH,
        )

    def v_copy(i):
        p = lax.rem(me + i, devices)
        return pltpu.make_async_remote_copy(
            fkv_hbm.at[:, pl.ds((chips + p // 2) * depth, depth)],
            vx.at[pl.ds(cached + me * rows, rows), pl.ds(0, depth)],
            v_send.at[i], v_recv.at[i], device_id={"sp": p}, device_id_type=MESH,
        )

    def l_copy(i):
        p = lax.rem(me + i, devices)
        return pltpu.make_async_remote_copy(
            lens_ref, lb.at[me], l_send.at[i], l_recv.at[i],
            device_id={"sp": p}, device_id_type=MESH,
        )

    def q_copy(p):
        return pltpu.make_async_remote_copy(
            q_hbm.at[:, pl.ds(p * wide, wide)], qb.at[me], q_send.at[p], q_recv.at[me],
            device_id={"sp": p}, device_id_type=MESH,
        )

    cache_copies = [
        pltpu.make_async_remote_copy(
            cache_hbm.at[:, pl.ds(d * depth, depth)],
            dst.at[pl.ds(c * block, block), pl.ds(0, depth)],
            c_send.at[d], c_recv.at[d], device_id={"sp": partner}, device_id_type=MESH,
        )
        for d, dst in enumerate((kx, vx))
    ]
    far_first = (4, 5, 3, 2, 6, 1, 7)
    for i in far_first:
        k_copy(i).start()
        v_copy(i).start()
        l_copy(i).start()
    for copy in cache_copies:
        copy.start()
    q_copy(partner).start()
    for dy in (2, 1, 3):
        for cc in range(2):
            q_copy(lax.rem(y + dy, chips) * 2 + cc).start()

    lanes = lax.broadcasted_iota(jnp.int32, (8, rows), 1)
    living = lanes < lens_ref[:, 0:1]
    expert_rows = lax.broadcasted_iota(jnp.int32, (experts, rows), 0)
    named = jnp.where(living, ids_ref[...], experts)
    routed = jnp.zeros((experts, rows), jnp.float32)
    for k in range(8):
        routed = routed + jnp.where(named[k : k + 1, :] == expert_rows, 1.0, 0.0)
    square = (rows, rows)
    before = jnp.where(
        lax.broadcasted_iota(jnp.int32, square, 0) < lax.broadcasted_iota(jnp.int32, square, 1),
        1.0,
        0.0,
    ).astype(jnp.bfloat16)
    prefix = jnp.dot(routed.astype(jnp.bfloat16), before, preferred_element_type=jnp.float32)
    info[0:8, :] = named.astype(jnp.float32)
    for k in range(8):
        hits = jnp.where(named[k : k + 1, :] == expert_rows, prefix, 0.0)
        info[8 + k : 9 + k, :] = jnp.sum(hits, axis=0, keepdims=True) + 1.0
    info[16:24, :] = gates_ref[...]

    for copy in local_copies:
        copy.wait()
    for copy in cache_copies:
        copy.wait_recv()
    for i in range(1, devices):
        l_copy(i).wait_recv()
        k_copy(i).wait_recv()
        v_copy(i).wait_recv()
    row_ids = lax.broadcasted_iota(jnp.int32, (rows, depth), 0)
    for t in range(devices):
        alive = row_ids < lb[t, 0:1, :]
        kx[cached + t * rows : cached + (t + 1) * rows, depth:] = jnp.where(
            alive, 0.0, NEG
        ).astype(jnp.bfloat16)

    scale = math.log2(math.e) / math.sqrt(depth)
    pair_rows = 2 * rows
    lane = lax.broadcasted_iota(jnp.int32, (pair_rows, depth), 1)
    pick = jnp.where(lane == 0, 1.0, 0.0).astype(jnp.bfloat16)

    def attend(chip):
        keys = cached + (chip + 1) * pair_rows
        first = (cached + chip * pair_rows) // 128 * 128
        shift = cached + chip * pair_rows - first

        def head(h, carry):
            q = qb[2 * chip : 2 * chip + 2, :, pl.ds(pl.multiple_of(h * depth, depth), depth)]
            q = jnp.concatenate([q.reshape(pair_rows, depth), pick], axis=1)
            dims = (((1,), (1,)), ((), ()))
            sa = lax.dot_general(q, kx[:first, :], dims, preferred_element_type=jnp.float32)
            sb = lax.dot_general(q, kx[first:keys, :], dims, preferred_element_type=jnp.float32)
            i = lax.broadcasted_iota(jnp.int32, sb.shape, 0)
            j = lax.broadcasted_iota(jnp.int32, sb.shape, 1)
            sb = jnp.where(j - shift <= i, sb, NEG)
            top = jnp.maximum(
                jnp.max(sa, axis=1, keepdims=True), jnp.max(sb, axis=1, keepdims=True)
            )
            pa = jnp.exp2((sa - top) * scale).astype(jnp.bfloat16)
            pb = jnp.exp2((sb - top) * scale).astype(jnp.bfloat16)
            out = jnp.dot(pa, vx[:first, :], preferred_element_type=jnp.float32)
            out = out + jnp.dot(pb, vx[first:keys, :], preferred_element_type=jnp.float32)
            heads[:, pl.ds(pl.multiple_of(h * depth, depth), depth)] = (
                out[:, :depth] / out[:, depth:]
            ).astype(jnp.bfloat16)
            return carry

        lax.fori_loop(0, per, head, 0)

    def pair_copy(slot):
        return pltpu.make_async_remote_copy(
            give.at[slot], take.at[slot], pair_send.at[slot], pair_recv.at[slot],
            device_id={"sp": partner}, device_id_type=MESH,
        )

    up = lax.rem(y + 1, chips) * 2 + c
    down = lax.rem(y + chips - 1, chips) * 2 + c

    def ring_copy(n):
        src, dst, to = (
            (relay.at[0, :, pl.ds(0, half)], half_in.at[0], up),
            (relay.at[0, :, pl.ds(half, half)], half_in.at[1], down),
            (relay.at[1], full_in.at[0], up),
            (relay.at[2], full_in.at[1], down),
        )[n]
        return pltpu.make_async_remote_copy(
            src, dst, ring_send.at[n], ring_recv.at[n],
            device_id={"sp": to}, device_id_type=MESH,
        )

    def project(side, store):
        mine = heads[pl.ds(pl.multiple_of(side * rows, rows), rows), :]
        for n in range(4):
            cols = slice(n * (width // 4), (n + 1) * (width // 4))
            store(cols, jnp.dot(mine, w[:, cols], preferred_element_type=jnp.float32))

    def step(n, carry):
        dy = jnp.where(n == 3, 3, lax.rem(n * 2, 3))
        chip = lax.rem(y + dy, chips)

        @pl.when(n > 0)
        def _():
            for cc in range(2):
                t = chip * 2 + cc
                pltpu.make_async_copy(qb.at[t], qb.at[t], q_recv.at[t]).wait()

        @pl.when(n == 0)
        def _():
            pltpu.make_async_copy(qb.at[partner], qb.at[partner], q_recv.at[partner]).wait()

        lax.switch(chip, [functools.partial(attend, k) for k in range(chips)])

        def to_give(cols, value):
            give[n, :, cols] = value.astype(jnp.bfloat16)

        def to_own(cols, value):
            own_part[n, :, cols] = value

        project(1 - c, to_give)
        pair_copy(n).start()
        project(c, to_own)

        @pl.when(n == 1)
        def _():
            pair_copy(1).wait_recv()
            relay[0] = (own_part[1] + take[1].astype(jnp.float32)).astype(jnp.bfloat16)
            ring_copy(0).start()
            ring_copy(1).start()

        @pl.when(n == 2)
        def _():
            pair_copy(2).wait_recv()
            ring_copy(0).wait_recv()
            relay[1, :, :half] = (
                own_part[2, :, :half]
                + take[2, :, :half].astype(jnp.float32)
                + half_in[0].astype(jnp.float32)
            ).astype(jnp.bfloat16)
            relay[1, :, half:] = (
                own_part[2, :, half:] + take[2, :, half:].astype(jnp.float32)
            ).astype(jnp.bfloat16)
            ring_copy(2).start()

        @pl.when(n == 3)
        def _():
            pair_copy(3).wait_recv()
            ring_copy(1).wait_recv()
            relay[2, :, :half] = (
                own_part[3, :, :half] + take[3, :, :half].astype(jnp.float32)
            ).astype(jnp.bfloat16)
            relay[2, :, half:] = (
                own_part[3, :, half:]
                + take[3, :, half:].astype(jnp.float32)
                + half_in[1].astype(jnp.float32)
            ).astype(jnp.bfloat16)
            ring_copy(3).start()

        return carry

    lax.fori_loop(0, chips, step, 0)
    pair_copy(0).wait_recv()
    own_part[0] = own_part[0] + take[0].astype(jnp.float32)
    ring_copy(2).wait_recv()
    own_part[0] = own_part[0] + full_in[0].astype(jnp.float32)
    ring_copy(3).wait_recv()
    total = own_part[0] + full_in[1].astype(jnp.float32)
    attended_ref[...] = total.astype(jnp.bfloat16)
    mixed = res[...].astype(jnp.float32) + total
    power = jnp.mean(mixed * mixed, axis=1, keepdims=True)
    normed_ref[...] = (mixed * lax.rsqrt(power + 1e-06) * gain_ref[...]).astype(jnp.bfloat16)

    for i in range(1, devices):
        k_copy(i).wait_send()
        v_copy(i).wait_send()
        l_copy(i).wait_send()
        q_copy(lax.rem(me + i, devices)).wait_send()
    for copy in cache_copies:
        copy.wait_send()
    for n in range(4):
        pair_copy(n).wait_send()
        ring_copy(n).wait_send()


def attention(
    queries, fresh_key_values, cache, lengths, out_weight, residual, norm_gain, expert_ids, gate_values
):
    experts = lax.axis_size("grp") * lax.axis_size("sp")
    top = expert_ids.shape[1]
    devices = lax.axis_size("sp")
    rows, wide = queries.shape[0], queries.shape[1] // devices
    block, depth = cache.shape[2], cache.shape[3] // 2
    width = residual.shape[1]
    keys = 2 * block + devices * rows
    any_spec = pl.BlockSpec(memory_space=pl.ANY)
    vmem = pl.BlockSpec(memory_space=pltpu.VMEM)
    dma = pltpu.SemaphoreType.DMA
    out = jax.ShapeDtypeStruct((rows, width), jnp.bfloat16)
    return pl.pallas_call(
        functools.partial(group_attention, experts),
        out_shape=(out, out, jax.ShapeDtypeStruct((3 * top, rows), jnp.float32)),
        in_specs=[any_spec, any_spec, any_spec, vmem, any_spec, any_spec, vmem, vmem, vmem],
        out_specs=(vmem, vmem, vmem),
        scratch_shapes=[
            pltpu.VMEM((devices, rows, wide), jnp.bfloat16),
            pltpu.VMEM((keys, 2 * depth), jnp.bfloat16),
            pltpu.VMEM((keys, 2 * depth), jnp.bfloat16),
            pltpu.VMEM((devices, 8, 128), jnp.int32),
            pltpu.VMEM(out_weight.shape, jnp.bfloat16),
            pltpu.VMEM((rows, width), jnp.bfloat16),
            pltpu.VMEM((2 * rows, wide), jnp.bfloat16),
            pltpu.VMEM((4, rows, width), jnp.float32),
            pltpu.VMEM((4, rows, width), jnp.bfloat16),
            pltpu.VMEM((4, rows, width), jnp.bfloat16),
            pltpu.VMEM((3, rows, width), jnp.bfloat16),
            pltpu.VMEM((2, rows, width // 2), jnp.bfloat16),
            pltpu.VMEM((2, rows, width), jnp.bfloat16),
            dma((devices,)), dma((devices,)), dma((devices,)), dma((devices,)),
            dma((devices,)), dma((devices,)), dma((devices,)), dma((devices,)),
            dma((2,)), dma((2,)), dma((8,)), dma((4,)), dma((4,)), dma((4,)), dma((4,)),
        ],
        compiler_params=pltpu.CompilerParams(
            collective_id=0, has_side_effects=True, vmem_limit_bytes=56 * 1024 * 1024
        ),
    )(
        queries,
        fresh_key_values,
        cache[0, 0],
        jnp.broadcast_to(lengths, (8, 128)),
        out_weight,
        residual,
        norm_gain[None, :],
        expert_ids.T,
        gate_values.T,
    )


SLOTS = 16


def expert_exchange(
    line, columns,
    normed_hbm, meta_hbm, up_hbm, down_hbm,
    out_ref,
    xg0, xg1, xg2, meta, sb0, sb1, sb2, rc0, rc1, rc2, rd0, rd1, rd2, rt0, rt1, rt2,
    rs0, rs1, rs2, pb0, pb1, pb2, up, down, hidden,
    w_sem, meta_send, meta_recv, x_send, x_recv, d_send, d_recv,
    r_send, r_recv, s_send, s_recv,
):
    xg, sb, rt = (xg0, xg1, xg2), (sb0, sb1, sb2), (rt0, rt1, rt2)
    rs, pb = (rs0, rs1, rs2), (pb0, pb1, pb2)
    recv, ready = (rc0, rc1, rc2), (rd0, rd1, rd2)
    grp, sp = lax.axis_index("grp"), lax.axis_index("sp")
    pos = (grp // line, sp // 2, lax.rem(grp, line))
    core = lax.rem(sp, 2)
    rows = meta.shape[3]
    plane = 2 * line * line
    ff, width = down.shape

    def wrap(value):
        return lax.rem(value + 2 * line, line)

    def device(p, cc):
        return (p[0] * line + p[2], p[1] * 2 + cc)

    def others(a):
        return (a + 1) % 3, (a + 2) % 3

    def moved(p, a, value):
        p = list(p)
        p[a] = value
        return p

    def source(group, a, p):
        i, j = others(a)
        return wrap(group - p[i] - p[j])

    def cols(a):
        return pl.ds(columns[a][0], columns[a][1])

    def span(a):
        return slice(columns[a][0], columns[a][0] + columns[a][1])

    bar = pltpu.get_barrier_semaphore()
    peers = [
        (dx, dy, dz, dc)
        for dx in range(line) for dy in range(line) for dz in range(line) for dc in range(2)
        if dx * dy * dz == 0 and (dx, dy, dz, dc) != (0, 0, 0, 0)
    ]
    for dx, dy, dz, dc in peers:
        p = (lax.rem(pos[0] + dx, line), lax.rem(pos[1] + dy, line), lax.rem(pos[2] + dz, line))
        pl.semaphore_signal(
            bar, inc=1, device_id=device(p, lax.rem(core + dc, 2)), device_id_type=MESH
        )
    weights = (
        pltpu.make_async_copy(up_hbm.at[0], up, w_sem.at[0]),
        pltpu.make_async_copy(down_hbm.at[0], down, w_sem.at[1]),
    )
    for copy in weights:
        copy.start()
    for a in range(3):
        pltpu.make_async_copy(meta_hbm, meta.at[a, pos[a]], meta_recv.at[a, pos[a]]).start()
        pltpu.make_async_copy(
            normed_hbm.at[:, cols(a)], xg[a].at[pos[a]], x_recv.at[a, pos[a]]
        ).start()
    pl.semaphore_wait(bar, len(peers))

    def meta_copy(a, k):
        to = device(moved(pos, a, lax.rem(pos[a] + k, line)), core)
        return pltpu.make_async_remote_copy(
            meta_hbm, meta.at[a, pos[a]], meta_send.at[a, k], meta_recv.at[a, pos[a]],
            device_id=to, device_id_type=MESH,
        )

    def x_copy(a, k):
        to = device(moved(pos, a, lax.rem(pos[a] + k, line)), core)
        return pltpu.make_async_remote_copy(
            normed_hbm.at[:, cols(a)], xg[a].at[pos[a]], x_send.at[a, k], x_recv.at[a, pos[a]],
            device_id=to, device_id_type=MESH,
        )

    hops = sorted(range(1, line), key=lambda k: (min(k, line - k), k))
    for k in hops:
        for a in range(3):
            meta_copy(a, k).start()

    def share_rows():
        for k in hops:
            for a in range(3):
                x_copy(a, k).start()

    group_mine = lax.rem(pos[0] + pos[1] + pos[2], line)
    share_rows()
    for a in range(3):
        for i in range(line):
            pltpu.make_async_copy(meta.at[a, i], meta.at[a, i], meta_recv.at[a, i]).wait()

    shift = line.bit_length() - 1
    q = lax.broadcasted_iota(jnp.int32, (plane, rows), 0)
    q_u = lax.shift_right_logical(q, shift + 1)
    q_v = lax.bitwise_and(lax.shift_right_logical(q, 1), line - 1)
    q_c = lax.bitwise_and(q, 1)
    big = (plane * SLOTS, plane)
    spread = jnp.where(
        lax.shift_right_logical(lax.broadcasted_iota(jnp.int32, big, 0), 4)
        == lax.broadcasted_iota(jnp.int32, big, 1),
        1.0,
        0.0,
    ).astype(jnp.bfloat16)
    slot = (
        lax.bitwise_and(lax.broadcasted_iota(jnp.int32, (plane * SLOTS, rows), 0), SLOTS - 1) + 1
    ).astype(jnp.float32)

    def routing(a, i, gated):
        u, v = others(a)
        where = [None, None, None]
        where[a], where[u], where[v] = pos[a], q_u, q_v
        expert = ((where[0] * line + where[2]) * line + where[1]) * 2 + q_c
        expert = expert.astype(jnp.float32)
        info = meta[a, i]
        place = jnp.zeros((plane, rows), jnp.float32)
        gate = jnp.zeros((plane, rows), jnp.float32)
        for k in range(8):
            match = info[k : k + 1, :] == expert
            place = place + jnp.where(match, info[8 + k : 9 + k, :], 0.0)
            if gated:
                gate = gate + jnp.where(match, info[16 + k : 17 + k, :], 0.0)
        hit = jnp.dot(spread, place.astype(jnp.bfloat16), preferred_element_type=jnp.float32) == slot
        if gated:
            value = jnp.dot(spread, gate.astype(jnp.bfloat16), preferred_element_type=jnp.float32)
        else:
            value = 1.0
        return jnp.where(hit, value, 0.0).astype(jnp.bfloat16)

    steps = [(0, 0)] + sorted(
        [(i, j) for i in range(line) for j in range(line) if (i, j) != (0, 0)],
        key=lambda o: (
            min(o[0], line - o[0]) + min(o[1], line - o[1]),
            sorted((min(o[0], line - o[0]), min(o[1], line - o[1]))),
        ),
    )

    def plane_peer(a, step, dc):
        u, v = others(a)
        p = moved(pos, u, lax.rem(pos[u] + step[0], line))
        p = moved(p, v, lax.rem(pos[v] + step[1], line))
        return p, lax.rem(core + dc, 2)

    def index_in_plane(a, p, cc):
        u, v = others(a)
        return (p[u] * line + p[v]) * 2 + cc

    def spots():
        for dc in range(2):
            for step in steps:
                for a in range(3):
                    yield a, step, dc

    def dispatch(group, carry):

        chosen = [routing(a, source(group, a, pos), False) for a in range(3)]
        for a in range(3):
            i = source(group, a, pos)
            pltpu.make_async_copy(xg[a].at[i], xg[a].at[i], x_recv.at[a, i]).wait()
            picked = jnp.dot(
                chosen[a], xg[a][i], preferred_element_type=jnp.float32
            ).astype(jnp.bfloat16)
            sb[a][group] = picked.reshape(plane, SLOTS, columns[a][1])
        for a, step, dc in spots():
            p, cc = plane_peer(a, step, dc)
            d = moved(pos, a, source(group, a, pos))
            src = sb[a].at[group, index_in_plane(a, p, cc)]
            dst = recv[a].at[group, d[0], d[2], core]
            if step == (0, 0) and dc == 0:
                pltpu.make_async_copy(src, dst, d_recv.at[a, group]).start()
            else:
                pltpu.make_async_remote_copy(
                    src, dst, d_send.at[a, group], d_recv.at[a, group],
                    device_id=device(p, cc), device_id_type=MESH,
                ).start()
        return carry

    lax.fori_loop(0, line, dispatch, 0)
    for copy in weights:
        copy.wait()

    block = min(256, ff)

    def experts(group, carry):
        for a in range(3):
            landed = recv[a].at[group]
            pltpu.make_async_copy(landed, landed, d_recv.at[a, group]).wait()

        def first(j, inner):
            x = jnp.concatenate(
                [recv[a][group].reshape(plane * SLOTS, columns[a][1]) for a in range(3)], axis=1
            )
            at = pl.multiple_of(j * block, block)
            gate = jnp.dot(x, up[:, pl.ds(at, block)], preferred_element_type=jnp.float32)
            lift = jnp.dot(x, up[:, pl.ds(ff + at, block)], preferred_element_type=jnp.float32)
            hidden[:, pl.ds(at, block)] = (gate / (1.0 + jnp.exp(-gate)) * lift).astype(jnp.bfloat16)
            return inner

        lax.fori_loop(0, ff // block, first, 0)

        for a in range(3):
            value = jnp.dot(hidden[...], down[:, span(a)], preferred_element_type=jnp.float32)
            ready[a][group] = value.astype(jnp.bfloat16).reshape(
                line, line, 2, SLOTS, columns[a][1]
            )
        for a, step, dc in spots():
            p, cc = plane_peer(a, step, dc)
            d = moved(p, a, source(group, a, p))
            src = ready[a].at[group, d[0], d[2], cc]
            dst = rt[a].at[group, index_in_plane(a, pos, core)]
            if step == (0, 0) and dc == 0:
                pltpu.make_async_copy(src, dst, r_recv.at[a, group]).start()
            else:
                pltpu.make_async_remote_copy(
                    src, dst, r_send.at[a, group], r_recv.at[a, group],
                    device_id=device(p, cc), device_id_type=MESH,
                ).start()
        return carry

    lax.fori_loop(0, line, experts, 0)

    def s_copy(a, i):
        to = device(moved(pos, a, i), core)
        return pltpu.make_async_remote_copy(
            pb[a].at[i], rs[a].at[pos[a]], s_send.at[a, i], s_recv.at[a, pos[a]],
            device_id=to, device_id_type=MESH,
        )

    def combine(group, carry):
        for a in range(3):
            i = source(group, a, pos)
            mixing = routing(a, i, True)
            pltpu.make_async_copy(rt[a].at[group], rt[a].at[group], r_recv.at[a, group]).wait()
            share = lax.dot_general(
                mixing,
                rt[a][group].reshape(plane * SLOTS, columns[a][1]),
                (((0,), (0,)), ((), ())),
                preferred_element_type=jnp.float32,
            )
            pb[a][i] = share.astype(jnp.bfloat16)

            @pl.when(i != pos[a])
            def _():
                s_copy(a, i).start()

        return carry

    lax.fori_loop(0, line, combine, 0)
    for a in range(3):
        total = pb[a][pos[a]].astype(jnp.float32)
        for k in range(1, line):
            i = lax.rem(pos[a] + k, line)
            pltpu.make_async_copy(rs[a].at[i], rs[a].at[i], s_recv.at[a, i]).wait()
            total = total + rs[a][i].astype(jnp.float32)
        out_ref[:, columns[a][0] : columns[a][0] + columns[a][1]] = total.astype(jnp.bfloat16)

    for a in range(3):
        for k in range(1, line):
            meta_copy(a, k).wait_send()
            x_copy(a, k).wait_send()
            s_copy(a, lax.rem(pos[a] + k, line)).wait_send()
        for group in range(line):
            sent = sb[a].at[group, pl.ds(0, plane - 1)]
            pltpu.make_async_copy(sent, sent, d_send.at[a, group]).wait()
            back = rt[a].at[group, pl.ds(0, plane - 1)]
            pltpu.make_async_copy(back, back, r_send.at[a, group]).wait()


def mix_experts(normed, meta, up_gate_weight, down_weight):
    line = math.isqrt(lax.axis_size("grp"))
    rows, width = normed.shape
    ff = down_weight.shape[1]
    plane = 2 * line * line
    tiles = width // 128
    cuts = [0, tiles // 3, 2 * (tiles // 3), tiles]
    columns = [(128 * cuts[a], 128 * (cuts[a + 1] - cuts[a])) for a in range(3)]
    any_spec = pl.BlockSpec(memory_space=pl.ANY)
    dma = pltpu.SemaphoreType.DMA

    def buffers(*shape):
        return [pltpu.VMEM((*shape, columns[a][1]), jnp.bfloat16) for a in range(3)]

    return pl.pallas_call(
        functools.partial(expert_exchange, line, columns),
        out_shape=jax.ShapeDtypeStruct((rows, width), jnp.bfloat16),
        in_specs=[any_spec] * 4,
        out_specs=pl.BlockSpec(memory_space=pltpu.VMEM),
        scratch_shapes=[
            *buffers(line, rows),
            pltpu.VMEM((3, line, *meta.shape), jnp.float32),
            *buffers(line, plane, SLOTS),
            *buffers(line, line, line, 2, SLOTS),
            *buffers(line, line, line, 2, SLOTS),
            *buffers(line, plane, SLOTS),
            *buffers(line, rows),
            *buffers(line, rows),
            pltpu.VMEM(up_gate_weight.shape[1:], jnp.bfloat16),
            pltpu.VMEM(down_weight.shape[1:], jnp.bfloat16),
            pltpu.VMEM((plane * SLOTS, ff), jnp.bfloat16),
            dma((2,)),
            dma((3, line)), dma((3, line)), dma((3, line)), dma((3, line)),
            dma((3, line)), dma((3, line)), dma((3, line)), dma((3, line)),
            dma((3, line)), dma((3, line)),
        ],
        compiler_params=pltpu.CompilerParams(
            collective_id=1, has_side_effects=True, vmem_limit_bytes=67_000_000
        ),
    )(normed, meta, up_gate_weight, down_weight)


def per_device(
    queries,
    fresh_key_values,
    cache,
    lengths,
    out_weight,
    residual,
    norm_gain,
    expert_ids,
    gate_values,
    up_gate_weight,
    down_weight,
):
    seq_devices = lax.axis_size("sp")
    slot_rows = queries.shape[0]
    attn_sum, normed, info = attention(
        queries, fresh_key_values, cache, lengths, out_weight, residual, norm_gain, expert_ids, gate_values
    )
    mixed = mix_experts(normed, info, up_gate_weight, down_weight)
    slots = jnp.arange(queries.shape[0], dtype=jnp.int32)
    own_live = (slots < lengths[0, 0])[:, None]
    zero = jnp.zeros((), jnp.bfloat16)
    return (jnp.where(own_live, attn_sum, zero), jnp.where(own_live, mixed, zero))


def solution(mesh):
    in_specs = (
        P(("grp", "sp"), None),
        P(("grp", "sp"), None),
        P("grp", "sp", None, None),
        P("grp", "sp"),
        P("sp", None),
        P(("grp", "sp"), None),
        P(),
        P(("grp", "sp"), None),
        P(("grp", "sp"), None),
        P(("grp", "sp"), None, None),
        P(("grp", "sp"), None, None),
    )
    out_specs = (P(("grp", "sp"), None), P(("grp", "sp"), None))
    return jax.shard_map(
        per_device, mesh=mesh, in_specs=in_specs, out_specs=out_specs, check_vma=False
    )
```

```python
import functools
import math

import jax
import jax.numpy as jnp
from jax import lax
from jax.experimental import pallas as pl
from jax.experimental.pallas import tpu as pltpu
from jax.sharding import PartitionSpec as P


MESH = pl.DeviceIdType.MESH
NEG = -1e30


def group_attention(
    experts,
    q_hbm, fkv_hbm, cache_hbm, lens_ref, w_hbm, res_hbm, gain_ref, ids_ref, gates_ref,
    attended_ref, normed_ref, info,
    qb, kx, vx, lb, w, res, heads, own_part, give, take, relay, half_in, full_in,
    q_send, k_send, v_send, l_send, q_recv, k_recv, v_recv, l_recv,
    c_send, c_recv, local, pair_send, pair_recv, ring_send, ring_recv,
):
    me = lax.axis_index("sp")
    devices = qb.shape[0]
    rows, wide = qb.shape[1], qb.shape[2]
    depth = kx.shape[1] // 2
    per = wide // depth
    block = cache_hbm.shape[0]
    cached = 2 * block
    chips = devices // 2
    y, c = me // 2, lax.rem(me, 2)
    partner = y * 2 + 1 - c
    width = w.shape[1]
    half = width // 2

    bar = pltpu.get_barrier_semaphore()
    for i in range(1, devices):
        pl.semaphore_signal(
            bar, inc=1, device_id={"sp": lax.rem(me + i, devices)}, device_id_type=MESH
        )

    local_copies = [
        pltpu.make_async_copy(w_hbm, w, local.at[0]),
        pltpu.make_async_copy(res_hbm, res, local.at[1]),
        pltpu.make_async_copy(
            cache_hbm.at[:, pl.ds(0, depth)],
            kx.at[pl.ds(c * block, block), pl.ds(0, depth)],
            local.at[2],
        ),
        pltpu.make_async_copy(
            cache_hbm.at[:, pl.ds(depth, depth)],
            vx.at[pl.ds(c * block, block), pl.ds(0, depth)],
            local.at[3],
        ),
        pltpu.make_async_copy(
            fkv_hbm.at[:, pl.ds(y * depth, depth)],
            kx.at[pl.ds(cached + me * rows, rows), pl.ds(0, depth)],
            local.at[4],
        ),
        pltpu.make_async_copy(
            fkv_hbm.at[:, pl.ds((chips + y) * depth, depth)],
            vx.at[pl.ds(cached + me * rows, rows), pl.ds(0, depth)],
            local.at[5],
        ),
        pltpu.make_async_copy(q_hbm.at[:, pl.ds(me * wide, wide)], qb.at[me], local.at[6]),
        pltpu.make_async_copy(lens_ref, lb.at[me], local.at[7]),
    ]
    for copy in local_copies:
        copy.start()

    vx[:, depth:] = jnp.ones((vx.shape[0], depth), jnp.bfloat16)
    kx[:cached, depth:] = jnp.zeros((cached, depth), jnp.bfloat16)

    pl.semaphore_wait(bar, devices - 1)

    def k_copy(i):
        p = lax.rem(me + i, devices)
        return pltpu.make_async_remote_copy(
            fkv_hbm.at[:, pl.ds((p // 2) * depth, depth)],
            kx.at[pl.ds(cached + me * rows, rows), pl.ds(0, depth)],
            k_send.at[i], k_recv.at[i], device_id={"sp": p}, device_id_type=MESH,
        )

    def v_copy(i):
        p = lax.rem(me + i, devices)
        return pltpu.make_async_remote_copy(
            fkv_hbm.at[:, pl.ds((chips + p // 2) * depth, depth)],
            vx.at[pl.ds(cached + me * rows, rows), pl.ds(0, depth)],
            v_send.at[i], v_recv.at[i], device_id={"sp": p}, device_id_type=MESH,
        )

    def l_copy(i):
        p = lax.rem(me + i, devices)
        return pltpu.make_async_remote_copy(
            lens_ref, lb.at[me], l_send.at[i], l_recv.at[i],
            device_id={"sp": p}, device_id_type=MESH,
        )

    def q_copy(p):
        return pltpu.make_async_remote_copy(
            q_hbm.at[:, pl.ds(p * wide, wide)], qb.at[me], q_send.at[p], q_recv.at[me],
            device_id={"sp": p}, device_id_type=MESH,
        )

    cache_copies = [
        pltpu.make_async_remote_copy(
            cache_hbm.at[:, pl.ds(d * depth, depth)],
            dst.at[pl.ds(c * block, block), pl.ds(0, depth)],
            c_send.at[d], c_recv.at[d], device_id={"sp": partner}, device_id_type=MESH,
        )
        for d, dst in enumerate((kx, vx))
    ]
    far_first = (4, 5, 3, 2, 6, 1, 7)
    for i in far_first:
        k_copy(i).start()
        v_copy(i).start()
        l_copy(i).start()
    for copy in cache_copies:
        copy.start()
    q_copy(partner).start()
    for dc in range(2):
        for dy in (2, 1, 3):
            q_copy(lax.rem(y + dy, chips) * 2 + lax.rem(c + dc, 2)).start()

    lanes = lax.broadcasted_iota(jnp.int32, (8, rows), 1)
    living = lanes < lens_ref[:, 0:1]
    expert_rows = lax.broadcasted_iota(jnp.int32, (experts, rows), 0)
    named = jnp.where(living, ids_ref[...], experts)
    routed = jnp.zeros((experts, rows), jnp.float32)
    for k in range(8):
        routed = routed + jnp.where(named[k : k + 1, :] == expert_rows, 1.0, 0.0)
    square = (rows, rows)
    before = jnp.where(
        lax.broadcasted_iota(jnp.int32, square, 0) < lax.broadcasted_iota(jnp.int32, square, 1),
        1.0,
        0.0,
    ).astype(jnp.bfloat16)
    prefix = jnp.dot(routed.astype(jnp.bfloat16), before, preferred_element_type=jnp.float32)
    info[0:8, :] = named.astype(jnp.float32)
    for k in range(8):
        hits = jnp.where(named[k : k + 1, :] == expert_rows, prefix, 0.0)
        info[8 + k : 9 + k, :] = jnp.sum(hits, axis=0, keepdims=True) + 1.0
    info[16:24, :] = gates_ref[...]

    for copy in local_copies:
        copy.wait()
    for copy in cache_copies:
        copy.wait_recv()
    for i in range(1, devices):
        l_copy(i).wait_recv()
        k_copy(i).wait_recv()
        v_copy(i).wait_recv()
    row_ids = lax.broadcasted_iota(jnp.int32, (rows, depth), 0)
    for t in range(devices):
        alive = row_ids < lb[t, 0:1, :]
        kx[cached + t * rows : cached + (t + 1) * rows, depth:] = jnp.where(
            alive, 0.0, NEG
        ).astype(jnp.bfloat16)

    scale = math.log2(math.e) / math.sqrt(depth)
    pair_rows = 2 * rows
    lane = lax.broadcasted_iota(jnp.int32, (pair_rows, depth), 1)
    pick = jnp.where(lane == 0, 1.0, 0.0).astype(jnp.bfloat16)

    def attend(chip):
        keys = cached + (chip + 1) * pair_rows
        first = (cached + chip * pair_rows) // 128 * 128
        shift = cached + chip * pair_rows - first

        def head(h, carry):
            q = qb[2 * chip : 2 * chip + 2, :, pl.ds(pl.multiple_of(h * depth, depth), depth)]
            q = jnp.concatenate([q.reshape(pair_rows, depth), pick], axis=1)
            dims = (((1,), (1,)), ((), ()))
            sa = lax.dot_general(q, kx[:first, :], dims, preferred_element_type=jnp.float32)
            sb = lax.dot_general(q, kx[first:keys, :], dims, preferred_element_type=jnp.float32)
            i = lax.broadcasted_iota(jnp.int32, sb.shape, 0)
            j = lax.broadcasted_iota(jnp.int32, sb.shape, 1)
            sb = jnp.where(j - shift <= i, sb, NEG)
            top = jnp.maximum(
                jnp.max(sa, axis=1, keepdims=True), jnp.max(sb, axis=1, keepdims=True)
            )
            pa = jnp.exp2((sa - top) * scale).astype(jnp.bfloat16)
            pb = jnp.exp2((sb - top) * scale).astype(jnp.bfloat16)
            out = jnp.dot(pa, vx[:first, :], preferred_element_type=jnp.float32)
            out = out + jnp.dot(pb, vx[first:keys, :], preferred_element_type=jnp.float32)
            heads[:, pl.ds(pl.multiple_of(h * depth, depth), depth)] = (
                out[:, :depth] / out[:, depth:]
            ).astype(jnp.bfloat16)
            return carry

        lax.fori_loop(0, per, head, 0)

    def pair_copy(slot):
        return pltpu.make_async_remote_copy(
            give.at[slot], take.at[slot], pair_send.at[slot], pair_recv.at[slot],
            device_id={"sp": partner}, device_id_type=MESH,
        )

    up = lax.rem(y + 1, chips) * 2 + c
    down = lax.rem(y + chips - 1, chips) * 2 + c

    def ring_copy(n):
        src, dst, to = (
            (relay.at[0, :, pl.ds(0, half)], half_in.at[0], up),
            (relay.at[0, :, pl.ds(half, half)], half_in.at[1], down),
            (relay.at[1], full_in.at[0], up),
            (relay.at[2], full_in.at[1], down),
        )[n]
        return pltpu.make_async_remote_copy(
            src, dst, ring_send.at[n], ring_recv.at[n],
            device_id={"sp": to}, device_id_type=MESH,
        )

    def project(side, store):
        mine = heads[pl.ds(pl.multiple_of(side * rows, rows), rows), :]
        for n in range(4):
            cols = slice(n * (width // 4), (n + 1) * (width // 4))
            store(cols, jnp.dot(mine, w[:, cols], preferred_element_type=jnp.float32))

    def step(n, carry):
        dy = jnp.where(n == 3, 3, lax.rem(n * 2, 3))
        chip = lax.rem(y + dy, chips)

        @pl.when(n > 0)
        def _():
            for cc in range(2):
                t = chip * 2 + cc
                pltpu.make_async_copy(qb.at[t], qb.at[t], q_recv.at[t]).wait()

        @pl.when(n == 0)
        def _():
            pltpu.make_async_copy(qb.at[partner], qb.at[partner], q_recv.at[partner]).wait()

        lax.switch(chip, [functools.partial(attend, k) for k in range(chips)])

        def to_give(cols, value):
            give[n, :, cols] = value.astype(jnp.bfloat16)

        def to_own(cols, value):
            own_part[n, :, cols] = value

        project(1 - c, to_give)
        pair_copy(n).start()
        project(c, to_own)

        @pl.when(n == 1)
        def _():
            pair_copy(1).wait_recv()
            relay[0] = (own_part[1] + take[1].astype(jnp.float32)).astype(jnp.bfloat16)
            ring_copy(0).start()
            ring_copy(1).start()

        @pl.when(n == 2)
        def _():
            pair_copy(2).wait_recv()
            ring_copy(0).wait_recv()
            relay[1, :, :half] = (
                own_part[2, :, :half]
                + take[2, :, :half].astype(jnp.float32)
                + half_in[0].astype(jnp.float32)
            ).astype(jnp.bfloat16)
            relay[1, :, half:] = (
                own_part[2, :, half:] + take[2, :, half:].astype(jnp.float32)
            ).astype(jnp.bfloat16)
            ring_copy(2).start()

        @pl.when(n == 3)
        def _():
            pair_copy(3).wait_recv()
            ring_copy(1).wait_recv()
            relay[2, :, :half] = (
                own_part[3, :, :half] + take[3, :, :half].astype(jnp.float32)
            ).astype(jnp.bfloat16)
            relay[2, :, half:] = (
                own_part[3, :, half:]
                + take[3, :, half:].astype(jnp.float32)
                + half_in[1].astype(jnp.float32)
            ).astype(jnp.bfloat16)
            ring_copy(3).start()

        return carry

    lax.fori_loop(0, chips, step, 0)
    pair_copy(0).wait_recv()
    own_part[0] = own_part[0] + take[0].astype(jnp.float32)
    ring_copy(2).wait_recv()
    own_part[0] = own_part[0] + full_in[0].astype(jnp.float32)
    ring_copy(3).wait_recv()
    total = own_part[0] + full_in[1].astype(jnp.float32)
    attended_ref[...] = total.astype(jnp.bfloat16)
    mixed = res[...].astype(jnp.float32) + total
    power = jnp.mean(mixed * mixed, axis=1, keepdims=True)
    normed_ref[...] = (mixed * lax.rsqrt(power + 1e-06) * gain_ref[...]).astype(jnp.bfloat16)

    for i in range(1, devices):
        k_copy(i).wait_send()
        v_copy(i).wait_send()
        l_copy(i).wait_send()
        q_copy(lax.rem(me + i, devices)).wait_send()
    for copy in cache_copies:
        copy.wait_send()
    for n in range(4):
        pair_copy(n).wait_send()
        ring_copy(n).wait_send()


def attention(
    queries, fresh_key_values, cache, lengths, out_weight, residual, norm_gain, expert_ids, gate_values
):
    experts = lax.axis_size("grp") * lax.axis_size("sp")
    top = expert_ids.shape[1]
    devices = lax.axis_size("sp")
    rows, wide = queries.shape[0], queries.shape[1] // devices
    block, depth = cache.shape[2], cache.shape[3] // 2
    width = residual.shape[1]
    keys = 2 * block + devices * rows
    any_spec = pl.BlockSpec(memory_space=pl.ANY)
    vmem = pl.BlockSpec(memory_space=pltpu.VMEM)
    dma = pltpu.SemaphoreType.DMA
    out = jax.ShapeDtypeStruct((rows, width), jnp.bfloat16)
    return pl.pallas_call(
        functools.partial(group_attention, experts),
        out_shape=(out, out, jax.ShapeDtypeStruct((3 * top, rows), jnp.float32)),
        in_specs=[any_spec, any_spec, any_spec, vmem, any_spec, any_spec, vmem, vmem, vmem],
        out_specs=(vmem, vmem, vmem),
        scratch_shapes=[
            pltpu.VMEM((devices, rows, wide), jnp.bfloat16),
            pltpu.VMEM((keys, 2 * depth), jnp.bfloat16),
            pltpu.VMEM((keys, 2 * depth), jnp.bfloat16),
            pltpu.VMEM((devices, 8, 128), jnp.int32),
            pltpu.VMEM(out_weight.shape, jnp.bfloat16),
            pltpu.VMEM((rows, width), jnp.bfloat16),
            pltpu.VMEM((2 * rows, wide), jnp.bfloat16),
            pltpu.VMEM((4, rows, width), jnp.float32),
            pltpu.VMEM((4, rows, width), jnp.bfloat16),
            pltpu.VMEM((4, rows, width), jnp.bfloat16),
            pltpu.VMEM((3, rows, width), jnp.bfloat16),
            pltpu.VMEM((2, rows, width // 2), jnp.bfloat16),
            pltpu.VMEM((2, rows, width), jnp.bfloat16),
            dma((devices,)), dma((devices,)), dma((devices,)), dma((devices,)),
            dma((devices,)), dma((devices,)), dma((devices,)), dma((devices,)),
            dma((2,)), dma((2,)), dma((8,)), dma((4,)), dma((4,)), dma((4,)), dma((4,)),
        ],
        compiler_params=pltpu.CompilerParams(
            collective_id=0, has_side_effects=True, vmem_limit_bytes=56 * 1024 * 1024
        ),
    )(
        queries,
        fresh_key_values,
        cache[0, 0],
        jnp.broadcast_to(lengths, (8, 128)),
        out_weight,
        residual,
        norm_gain[None, :],
        expert_ids.T,
        gate_values.T,
    )


SLOTS = 16


def expert_exchange(
    line, columns,
    normed_hbm, meta_hbm, up_hbm, down_hbm,
    out_ref,
    xg0, xg1, xg2, meta, sb0, sb1, sb2, rc0, rc1, rc2, rd0, rd1, rd2, rt0, rt1, rt2,
    rs0, rs1, rs2, pb0, pb1, pb2, up, down, hidden,
    w_sem, meta_send, meta_recv, x_send, x_recv, d_send, d_recv,
    r_send, r_recv, s_send, s_recv,
):
    xg, sb, rt = (xg0, xg1, xg2), (sb0, sb1, sb2), (rt0, rt1, rt2)
    rs, pb = (rs0, rs1, rs2), (pb0, pb1, pb2)
    recv, ready = (rc0, rc1, rc2), (rd0, rd1, rd2)
    grp, sp = lax.axis_index("grp"), lax.axis_index("sp")
    pos = (grp // line, sp // 2, lax.rem(grp, line))
    core = lax.rem(sp, 2)
    rows = meta.shape[3]
    plane = 2 * line * line
    ff, width = down.shape

    def wrap(value):
        return lax.rem(value + 2 * line, line)

    def device(p, cc):
        return (p[0] * line + p[2], p[1] * 2 + cc)

    def others(a):
        return (a + 1) % 3, (a + 2) % 3

    def moved(p, a, value):
        p = list(p)
        p[a] = value
        return p

    def source(group, a, p):
        i, j = others(a)
        return wrap(group - p[i] - p[j])

    def cols(a):
        return pl.ds(columns[a][0], columns[a][1])

    def span(a):
        return slice(columns[a][0], columns[a][0] + columns[a][1])

    bar = pltpu.get_barrier_semaphore()
    peers = [
        (dx, dy, dz, dc)
        for dx in range(line) for dy in range(line) for dz in range(line) for dc in range(2)
        if dx * dy * dz == 0 and (dx, dy, dz, dc) != (0, 0, 0, 0)
    ]
    for dx, dy, dz, dc in peers:
        p = (lax.rem(pos[0] + dx, line), lax.rem(pos[1] + dy, line), lax.rem(pos[2] + dz, line))
        pl.semaphore_signal(
            bar, inc=1, device_id=device(p, lax.rem(core + dc, 2)), device_id_type=MESH
        )
    weights = (
        pltpu.make_async_copy(up_hbm.at[0], up, w_sem.at[0]),
        pltpu.make_async_copy(down_hbm.at[0], down, w_sem.at[1]),
    )
    for copy in weights:
        copy.start()
    for a in range(3):
        pltpu.make_async_copy(meta_hbm, meta.at[a, pos[a]], meta_recv.at[a, pos[a]]).start()
        pltpu.make_async_copy(
            normed_hbm.at[:, cols(a)], xg[a].at[pos[a]], x_recv.at[a, pos[a]]
        ).start()
    pl.semaphore_wait(bar, len(peers))

    def meta_copy(a, k):
        to = device(moved(pos, a, lax.rem(pos[a] + k, line)), core)
        return pltpu.make_async_remote_copy(
            meta_hbm, meta.at[a, pos[a]], meta_send.at[a, k], meta_recv.at[a, pos[a]],
            device_id=to, device_id_type=MESH,
        )

    def x_copy(a, k):
        to = device(moved(pos, a, lax.rem(pos[a] + k, line)), core)
        return pltpu.make_async_remote_copy(
            normed_hbm.at[:, cols(a)], xg[a].at[pos[a]], x_send.at[a, k], x_recv.at[a, pos[a]],
            device_id=to, device_id_type=MESH,
        )

    hops = sorted(range(1, line), key=lambda k: (min(k, line - k), k))
    for k in hops:
        for a in range(3):
            meta_copy(a, k).start()

    def share_rows():
        for k in hops:
            for a in range(3):
                x_copy(a, k).start()

    group_mine = lax.rem(pos[0] + pos[1] + pos[2], line)
    share_rows()
    for a in range(3):
        for i in range(line):
            pltpu.make_async_copy(meta.at[a, i], meta.at[a, i], meta_recv.at[a, i]).wait()

    shift = line.bit_length() - 1
    q = lax.broadcasted_iota(jnp.int32, (plane, rows), 0)
    q_u = lax.shift_right_logical(q, shift + 1)
    q_v = lax.bitwise_and(lax.shift_right_logical(q, 1), line - 1)
    q_c = lax.bitwise_and(q, 1)
    big = (plane * SLOTS, plane)
    spread = jnp.where(
        lax.shift_right_logical(lax.broadcasted_iota(jnp.int32, big, 0), 4)
        == lax.broadcasted_iota(jnp.int32, big, 1),
        1.0,
        0.0,
    ).astype(jnp.bfloat16)
    slot = (
        lax.bitwise_and(lax.broadcasted_iota(jnp.int32, (plane * SLOTS, rows), 0), SLOTS - 1) + 1
    ).astype(jnp.float32)

    def routing(a, i, gated):
        u, v = others(a)
        where = [None, None, None]
        where[a], where[u], where[v] = pos[a], q_u, q_v
        expert = ((where[0] * line + where[2]) * line + where[1]) * 2 + q_c
        expert = expert.astype(jnp.float32)
        info = meta[a, i]
        place = jnp.zeros((plane, rows), jnp.float32)
        gate = jnp.zeros((plane, rows), jnp.float32)
        for k in range(8):
            match = info[k : k + 1, :] == expert
            place = place + jnp.where(match, info[8 + k : 9 + k, :], 0.0)
            if gated:
                gate = gate + jnp.where(match, info[16 + k : 17 + k, :], 0.0)
        hit = jnp.dot(spread, place.astype(jnp.bfloat16), preferred_element_type=jnp.float32) == slot
        if gated:
            value = jnp.dot(spread, gate.astype(jnp.bfloat16), preferred_element_type=jnp.float32)
        else:
            value = 1.0
        return jnp.where(hit, value, 0.0).astype(jnp.bfloat16)

    steps = [(0, 0)] + sorted(
        [(i, j) for i in range(line) for j in range(line) if (i, j) != (0, 0)],
        key=lambda o: (
            min(o[0], line - o[0]) + min(o[1], line - o[1]),
            sorted((min(o[0], line - o[0]), min(o[1], line - o[1]))),
        ),
    )

    def plane_peer(a, step, dc):
        u, v = others(a)
        p = moved(pos, u, lax.rem(pos[u] + step[0], line))
        p = moved(p, v, lax.rem(pos[v] + step[1], line))
        return p, lax.rem(core + dc, 2)

    def index_in_plane(a, p, cc):
        u, v = others(a)
        return (p[u] * line + p[v]) * 2 + cc

    def spots():
        for dc in range(2):
            for step in steps:
                for a in range(3):
                    yield a, step, dc

    def dispatch(group, carry):

        chosen = [routing(a, source(group, a, pos), False) for a in range(3)]
        for a in range(3):
            i = source(group, a, pos)
            pltpu.make_async_copy(xg[a].at[i], xg[a].at[i], x_recv.at[a, i]).wait()
            picked = jnp.dot(
                chosen[a], xg[a][i], preferred_element_type=jnp.float32
            ).astype(jnp.bfloat16)
            sb[a][group] = picked.reshape(plane, SLOTS, columns[a][1])
        for a, step, dc in spots():
            p, cc = plane_peer(a, step, dc)
            d = moved(pos, a, source(group, a, pos))
            src = sb[a].at[group, index_in_plane(a, p, cc)]
            dst = recv[a].at[group, d[0], d[2], core]
            if step == (0, 0) and dc == 0:
                pltpu.make_async_copy(src, dst, d_recv.at[a, group]).start()
            else:
                pltpu.make_async_remote_copy(
                    src, dst, d_send.at[a, group], d_recv.at[a, group],
                    device_id=device(p, cc), device_id_type=MESH,
                ).start()
        return carry

    lax.fori_loop(0, line, dispatch, 0)
    for copy in weights:
        copy.wait()

    block = min(256, ff)

    def experts(group, carry):
        for a in range(3):
            landed = recv[a].at[group]
            pltpu.make_async_copy(landed, landed, d_recv.at[a, group]).wait()

        def first(j, inner):
            x = jnp.concatenate(
                [recv[a][group].reshape(plane * SLOTS, columns[a][1]) for a in range(3)], axis=1
            )
            at = pl.multiple_of(j * block, block)
            gate = jnp.dot(x, up[:, pl.ds(at, block)], preferred_element_type=jnp.float32)
            lift = jnp.dot(x, up[:, pl.ds(ff + at, block)], preferred_element_type=jnp.float32)
            hidden[:, pl.ds(at, block)] = (gate / (1.0 + jnp.exp(-gate)) * lift).astype(jnp.bfloat16)
            return inner

        lax.fori_loop(0, ff // block, first, 0)

        for a in range(3):
            value = jnp.dot(hidden[...], down[:, span(a)], preferred_element_type=jnp.float32)
            ready[a][group] = value.astype(jnp.bfloat16).reshape(
                line, line, 2, SLOTS, columns[a][1]
            )
        for a, step, dc in spots():
            p, cc = plane_peer(a, step, dc)
            d = moved(p, a, source(group, a, p))
            src = ready[a].at[group, d[0], d[2], cc]
            dst = rt[a].at[group, index_in_plane(a, pos, core)]
            if step == (0, 0) and dc == 0:
                pltpu.make_async_copy(src, dst, r_recv.at[a, group]).start()
            else:
                pltpu.make_async_remote_copy(
                    src, dst, r_send.at[a, group], r_recv.at[a, group],
                    device_id=device(p, cc), device_id_type=MESH,
                ).start()
        return carry

    lax.fori_loop(0, line, experts, 0)

    def s_copy(a, i):
        to = device(moved(pos, a, i), core)
        return pltpu.make_async_remote_copy(
            pb[a].at[i], rs[a].at[pos[a]], s_send.at[a, i], s_recv.at[a, pos[a]],
            device_id=to, device_id_type=MESH,
        )

    def combine(group, carry):
        for a in range(3):
            i = source(group, a, pos)
            mixing = routing(a, i, True)
            pltpu.make_async_copy(rt[a].at[group], rt[a].at[group], r_recv.at[a, group]).wait()
            share = lax.dot_general(
                mixing,
                rt[a][group].reshape(plane * SLOTS, columns[a][1]),
                (((0,), (0,)), ((), ())),
                preferred_element_type=jnp.float32,
            )
            pb[a][i] = share.astype(jnp.bfloat16)

            @pl.when(i != pos[a])
            def _():
                s_copy(a, i).start()

        return carry

    lax.fori_loop(0, line, combine, 0)
    for a in range(3):
        total = pb[a][pos[a]].astype(jnp.float32)
        for k in range(1, line):
            i = lax.rem(pos[a] + k, line)
            pltpu.make_async_copy(rs[a].at[i], rs[a].at[i], s_recv.at[a, i]).wait()
            total = total + rs[a][i].astype(jnp.float32)
        out_ref[:, columns[a][0] : columns[a][0] + columns[a][1]] = total.astype(jnp.bfloat16)

    for a in range(3):
        for k in range(1, line):
            meta_copy(a, k).wait_send()
            x_copy(a, k).wait_send()
            s_copy(a, lax.rem(pos[a] + k, line)).wait_send()
        for group in range(line):
            sent = sb[a].at[group, pl.ds(0, plane - 1)]
            pltpu.make_async_copy(sent, sent, d_send.at[a, group]).wait()
            back = rt[a].at[group, pl.ds(0, plane - 1)]
            pltpu.make_async_copy(back, back, r_send.at[a, group]).wait()


def mix_experts(normed, meta, up_gate_weight, down_weight):
    line = math.isqrt(lax.axis_size("grp"))
    rows, width = normed.shape
    ff = down_weight.shape[1]
    plane = 2 * line * line
    tiles = width // 128
    cuts = [0, tiles // 3, 2 * (tiles // 3), tiles]
    columns = [(128 * cuts[a], 128 * (cuts[a + 1] - cuts[a])) for a in range(3)]
    any_spec = pl.BlockSpec(memory_space=pl.ANY)
    dma = pltpu.SemaphoreType.DMA

    def buffers(*shape):
        return [pltpu.VMEM((*shape, columns[a][1]), jnp.bfloat16) for a in range(3)]

    return pl.pallas_call(
        functools.partial(expert_exchange, line, columns),
        out_shape=jax.ShapeDtypeStruct((rows, width), jnp.bfloat16),
        in_specs=[any_spec] * 4,
        out_specs=pl.BlockSpec(memory_space=pltpu.VMEM),
        scratch_shapes=[
            *buffers(line, rows),
            pltpu.VMEM((3, line, *meta.shape), jnp.float32),
            *buffers(line, plane, SLOTS),
            *buffers(line, line, line, 2, SLOTS),
            *buffers(line, line, line, 2, SLOTS),
            *buffers(line, plane, SLOTS),
            *buffers(line, rows),
            *buffers(line, rows),
            pltpu.VMEM(up_gate_weight.shape[1:], jnp.bfloat16),
            pltpu.VMEM(down_weight.shape[1:], jnp.bfloat16),
            pltpu.VMEM((plane * SLOTS, ff), jnp.bfloat16),
            dma((2,)),
            dma((3, line)), dma((3, line)), dma((3, line)), dma((3, line)),
            dma((3, line)), dma((3, line)), dma((3, line)), dma((3, line)),
            dma((3, line)), dma((3, line)),
        ],
        compiler_params=pltpu.CompilerParams(
            collective_id=1, has_side_effects=True, vmem_limit_bytes=67_000_000
        ),
    )(normed, meta, up_gate_weight, down_weight)


def per_device(
    queries,
    fresh_key_values,
    cache,
    lengths,
    out_weight,
    residual,
    norm_gain,
    expert_ids,
    gate_values,
    up_gate_weight,
    down_weight,
):
    seq_devices = lax.axis_size("sp")
    slot_rows = queries.shape[0]
    attn_sum, normed, info = attention(
        queries, fresh_key_values, cache, lengths, out_weight, residual, norm_gain, expert_ids, gate_values
    )
    mixed = mix_experts(normed, info, up_gate_weight, down_weight)
    slots = jnp.arange(queries.shape[0], dtype=jnp.int32)
    own_live = (slots < lengths[0, 0])[:, None]
    zero = jnp.zeros((), jnp.bfloat16)
    return (jnp.where(own_live, attn_sum, zero), jnp.where(own_live, mixed, zero))


def solution(mesh):
    in_specs = (
        P(("grp", "sp"), None),
        P(("grp", "sp"), None),
        P("grp", "sp", None, None),
        P("grp", "sp"),
        P("sp", None),
        P(("grp", "sp"), None),
        P(),
        P(("grp", "sp"), None),
        P(("grp", "sp"), None),
        P(("grp", "sp"), None, None),
        P(("grp", "sp"), None, None),
    )
    out_specs = (P(("grp", "sp"), None), P(("grp", "sp"), None))
    return jax.shard_map(
        per_device, mesh=mesh, in_specs=in_specs, out_specs=out_specs, check_vma=False
    )
```
